256 devices in a mesh: head: 8 (over z), seq: 32 (over y, x, core).
Axes of the slice: x: 4, y: 4, z: 8, core: 2. Of those that a mesh axis runs over, the one named last changes fastest.
Arguments:
- tokens: bfloat16 [32768, 4096], P('seq')
- qkv_weight: bfloat16 [4096, 6144], P('seq', 'head'), may hold values from -0.09375 to 0.09375
- out_weight: bfloat16 [2048, 4096], P('head', 'seq'), may hold values from -0.125 to 0.125
- centroids: float32 [16, 256, 128], P('head', 'seq'), may hold values from -6 to 6
- clusters: int32 [16, 256], P('head', 'seq'), may hold values from 0 to 255, as said below
- slots: int32 [16, 256], P('head', 'seq'), may hold values from 0 to 1, as said below
Outputs:
- output: bfloat16 [4096, 32768], P('head', 'seq')
- new_centroids: float32 [16, 256, 128], P('head', 'seq')
The draws below stay inside these ranges and needn't reach their ends.
Inputs may be any that keep to these rules, and one draw needn't show every extreme that they name: `clusters`: for each head at most 2 tiles name one cluster, and in each head every cluster of some owner holds 2 tiles; the owner of cluster c is the index c // 8 of seq. A tile of head h from the index s of seq names an owner o with s + o - h divisible by 2. The tiles of one index of seq, over the 2 heads of one index of head, name pairwise different owners. Tiles of one head naming the same cluster have different slots.
All inputs are finite; a program needn't handle non-finite values.
Results may differ from the reference program's by a relative error of at most 0.017.
Values may be sent and summed in bfloat16 or wider, within the bound.
A program may use at most 128 MiB of HBM per device.

```python
import math
import jax
import jax.numpy as jnp
from jax import lax

D = 4096
HEAD_WIDTH = 128
HEAD_DEV = 2
TILE = 128
CAP = 2
TOK_DEV = 1024
HEADS = 16
CLUS_DEV = 8
CLUSTERS = 256
TOKENS = 32768
NT = 256
N_HEAD = 8
N_SEQ = 32


def routing_tables(key):
    key = jax.random.fold_in(key, 11)
    first_key, second_key, third_key, fourth_key = jax.random.split(key, 4)
    members = N_SEQ // HEAD_DEV
    tiles_dev = TOK_DEV // TILE
    local_head = jnp.arange(HEADS, dtype=jnp.int32) % HEAD_DEV
    source = jnp.arange(N_SEQ, dtype=jnp.int32)
    full_owner = jax.random.randint(first_key, (HEADS,), 0, N_SEQ)
    full_owner = jnp.where(jnp.arange(HEADS, dtype=jnp.int32) == 0, N_SEQ - 1, full_owner).astype(jnp.int32)
    residue = (local_head[:, None] - source[None, :]) % HEAD_DEV
    ranking = jax.random.randint(second_key, (HEADS, N_SEQ, members), 0, 1 << 20) * members + jnp.arange(members, dtype=jnp.int32)
    holds_full = residue == (full_owner % HEAD_DEV)[:, None]
    is_full = holds_full[:, :, None] & (jnp.arange(members, dtype=jnp.int32)[None, None, :] == (full_owner // HEAD_DEV)[:, None, None])
    ranking = jnp.where(is_full, 1 << 30, ranking)
    unused, chosen = lax.top_k(ranking, tiles_dev)
    shuffle = jnp.argsort(jax.random.randint(third_key, (HEADS, N_SEQ, tiles_dev), 0, 1 << 20) * tiles_dev + jnp.arange(tiles_dev, dtype=jnp.int32), axis=-1)
    chosen = jnp.take_along_axis(chosen, shuffle, axis=-1)
    owner = residue[:, :, None] + HEAD_DEV * chosen
    sigma = jnp.argsort(jax.random.randint(fourth_key, (HEADS, N_SEQ, members), 0, 1 << 20) * members + jnp.arange(members, dtype=jnp.int32), axis=-1)
    source_rank = (source // HEAD_DEV)[None, :, None]
    flat_index = (owner * members + source_rank).reshape(HEADS, N_SEQ * tiles_dev)
    placed = jnp.take_along_axis(sigma.reshape(HEADS, N_SEQ * members), flat_index, axis=1)
    cluster_ids = owner.reshape(HEADS, N_SEQ * tiles_dev) * CLUS_DEV + placed // CAP
    slot_ids = placed % CAP
    return (cluster_ids.astype(jnp.int32), slot_ids.astype(jnp.int32))


def draw_clusters(key, part):
    return routing_tables(key)[0]


def draw_slots(key, part):
    return routing_tables(key)[1]


def draw_tokens(key, part):
    key = jax.random.fold_in(key, 5)
    first_key, second_key, third_key, fourth_key = jax.random.split(key, 4)
    noise = jax.random.normal(first_key, (TOKENS, D), jnp.float32)
    common = jax.random.normal(second_key, (TOKENS // TILE, D), jnp.float32)
    row_scale = jnp.exp(jax.random.uniform(third_key, (TOKENS, 1), jnp.float32) * math.log(10.0))
    column_scale = jnp.exp(jax.random.uniform(fourth_key, (1, D), jnp.float32) * math.log(10.0))
    values = (noise + jnp.repeat(common, TILE, axis=0)) * row_scale * column_scale
    return values.astype(jnp.bfloat16)


def block_scale(stream_key, dims, shards, least, largest):
    loudness = 1.0
    for dim, shards_of in shards:
        draws = jax.random.uniform(jax.random.fold_in(jax.random.fold_in(stream_key, 6), dim), (shards_of,), jnp.float32, least / len(shards), largest / len(shards))
        loudness = loudness * jnp.repeat(jnp.exp(draws), dims[dim] // shards_of).reshape((-1,) + (1,) * (len(dims) - 1 - dim))
    return loudness


def scatter_about(stream_key, extent, deviation, most, pieces=(), held_as=jnp.bfloat16):
    level = block_scale(stream_key, extent, pieces, -0.22, 0.18) if pieces else 1.0
    result = jax.random.normal(stream_key, extent, jnp.float32) * deviation * level
    return jnp.minimum(jnp.maximum(result, -most), most).astype(held_as)


def setup_inputs(seed: int = 0) -> dict:
    streams_of = jax.random.split(jax.random.key(seed), 7)
    return {
        "tokens": draw_tokens(jax.random.fold_in(streams_of[6], 71), 0),
        "qkv_weight": scatter_about(streams_of[1], (D, HEADS * 3 * HEAD_WIDTH), D ** -0.5, 0.09375, ((0, 32), (1, 8))),
        "out_weight": scatter_about(streams_of[2], (HEADS * HEAD_WIDTH, D), (HEADS * HEAD_WIDTH) ** -0.5, 0.125, ((0, 8), (1, 32))),
        "centroids": scatter_about(streams_of[3], (HEADS, CLUSTERS, HEAD_WIDTH), 1.0, 6.0, ((0, 8), (1, 32)), jnp.float32),
        "clusters": draw_clusters(jax.random.fold_in(streams_of[6], 71), 0),
        "slots": draw_slots(jax.random.fold_in(streams_of[6], 71), 0),
    }


LOGIT_SCALE = 8.0
KEEP_RATE = 0.75

def unit_rows(values, epsilon):
    return values * lax.rsqrt(lax.optimization_barrier(jnp.mean(values * values, axis=-1, keepdims=True)) + epsilon)

def cluster_attention(normalized_query, normalized_key, value_matrix, token_live, position):
    attention_logits = LOGIT_SCALE / HEAD_WIDTH * jnp.einsum('tra,tla->trl', normalized_query.astype(jnp.float32), normalized_key.astype(jnp.float32))
    span_rows = normalized_query.shape[1]
    diagonal = jnp.arange(span_rows)[:, None] == jnp.arange(span_rows)[None, :]
    allowed = (token_live[:, None, :] > 0) & (position[:, None, :] <= position[:, :, None]) | diagonal[None]
    exp_scores = jnp.where(allowed, jnp.exp(attention_logits), 0.0)
    attention_probs = (exp_scores / lax.optimization_barrier(jnp.sum(exp_scores, axis=-1, keepdims=True))).astype(jnp.bfloat16)
    return jnp.einsum('xjs,xsv->xjv', attention_probs.astype(jnp.float32), value_matrix.astype(jnp.float32)).astype(jnp.bfloat16)

def update_centroids(centroid_rows, key_float, token_live, tiles_held):
    key_sums = lax.optimization_barrier(jnp.sum(key_float * token_live[:, :, None], axis=1))
    counts = tiles_held * TILE
    means = key_sums / jnp.maximum(counts, 1.0)[:, None]
    return centroid_rows + (1.0 - KEEP_RATE) * jnp.where(counts[:, None] > 0, means - centroid_rows, 0.0)

def head_pass(packed):
    qkv_head, cluster_ids, slot_ids, centroid_rows = packed
    slot_index = (cluster_ids * CAP + slot_ids).astype(jnp.int32)
    total_slots = CLUSTERS * CAP
    buffer = jnp.zeros((total_slots, TILE, 3, HEAD_WIDTH), jnp.bfloat16).at[slot_index].set(qkv_head)
    occupied = jnp.zeros((total_slots,), jnp.float32).at[slot_index].set(1.0)
    tile_of = jnp.zeros((total_slots,), jnp.int32).at[slot_index].set(jnp.arange(NT, dtype=jnp.int32))
    cluster_grouped_rows = buffer.reshape(CLUSTERS, CAP * TILE, 3, HEAD_WIDTH)
    token_live = jnp.repeat(occupied.reshape(CLUSTERS, CAP), TILE, axis=1)
    position = (tile_of.reshape(CLUSTERS, CAP, 1) * TILE + jnp.arange(TILE, dtype=jnp.int32)[None, None, :]).reshape(CLUSTERS, CAP * TILE)
    normalized_query = unit_rows(cluster_grouped_rows[:, :, 0].astype(jnp.float32), 1e-06).astype(jnp.bfloat16)
    key_float = unit_rows(cluster_grouped_rows[:, :, 1].astype(jnp.float32), 1e-06)
    normalized_key = key_float.astype(jnp.bfloat16)
    attended = cluster_attention(normalized_query, normalized_key, cluster_grouped_rows[:, :, 2], token_live, position)
    gathered_back = attended.reshape(total_slots, TILE, HEAD_WIDTH)[slot_index]
    tiles_held = lax.optimization_barrier(jnp.sum(occupied.reshape(CLUSTERS, CAP), axis=1))
    new_rows = update_centroids(centroid_rows, key_float, token_live, tiles_held)
    return (gathered_back, new_rows)

def add_group(running, packed):
    group_attention, group_weight = packed
    partial_value = jnp.dot(group_weight.T, group_attention.T, preferred_element_type=jnp.float32).astype(jnp.bfloat16)
    partial_value = lax.optimization_barrier(partial_value)
    return (running + partial_value.astype(jnp.float32), None)

def reference(tokens, qkv_weight, out_weight, centroids, clusters, slots):
    normed = unit_rows(tokens.astype(jnp.float32), 1e-05).astype(jnp.bfloat16)
    projected = jnp.dot(normed, qkv_weight, preferred_element_type=jnp.float32).astype(jnp.bfloat16)
    per_head = projected.reshape(NT, TILE, HEADS, 3, HEAD_WIDTH).transpose(2, 0, 1, 3, 4)
    attended, new_centroids = lax.map(head_pass, (per_head, clusters, slots, centroids))
    attention = attended.transpose(1, 2, 0, 3).reshape(TOKENS, HEADS * HEAD_WIDTH)
    group_width = HEADS * HEAD_WIDTH // N_HEAD
    grouped_attention = attention.reshape(TOKENS, N_HEAD, group_width).transpose(1, 0, 2)
    grouped_weight = out_weight.reshape(N_HEAD, group_width, D)
    running, unused = lax.scan(add_group, jnp.zeros((D, TOKENS), jnp.float32), (grouped_attention, grouped_weight))
    return (running.astype(jnp.bfloat16), new_centroids)
```

```python
import functools

import jax
import jax.numpy as jnp
from jax import lax
from jax.experimental import pallas as pl
from jax.experimental.pallas import tpu as pltpu
from jax.sharding import PartitionSpec as P

MESH = pl.DeviceIdType.MESH
F32 = jnp.float32
BF16 = jnp.bfloat16

NX = 4
NZ = 8
NCHIP = 16
NSEQ = 32
TILE = 128
TILES = 8
HW = 128
QKV = 3 * HW
WROWS = 128
OROWS = 64
OCOLS = 512
LOG2E = 1.4426950408889634
LOGIT = 8.0 / 128


def kernel(
    codes_ref, tok_hbm, w_ref, wo_ref, cent_ref,
    out_ref, newc_ref,
    tok, wbuf, obuf, owt, rscale,
    qkv0, qkv1, stage0, stage1, recv0, recv1, ret0, ret1, back0, back1,
    gbuf, acc, ksum,
    t_inv, t_lab, t_tile, t_par, t_lim, t_dst,
    tok_sem, w_send, w_recv, o_send, o_recv, sc_send, sc_recv, loc_sem,
    a_send, a_recv, r_send, r_recv, z_send, z_recv,
):
    z = lax.axis_index("head")
    s = lax.axis_index("seq")
    c = s % 2
    q = s // 2
    x = q % NX
    y = q // NX
    u = y * (1 - c) + x * c
    v = x * (1 - c) + y * c
    qkv = (qkv0, qkv1)
    stage = (stage0, stage1)
    recv = (recv0, recv1)
    ret = (ret0, ret1)
    back = (back0, back1)

    for t in range(TILES):
        pltpu.make_async_copy(
            tok_hbm.at[pl.ds(t * TILE, TILE)], tok.at[pl.ds(t * TILE, TILE)], tok_sem.at[t]
        ).start()
    own_w = pl.ds(pl.multiple_of(s * WROWS, WROWS), WROWS)
    wbuf[own_w, :] = w_ref[...]

    zg = s // 4
    barrier = pltpu.get_barrier_semaphore()

    def greet(i, carry):
        pl.semaphore_signal(barrier, inc=1, device_id=(z, (s + i) % NSEQ), device_id_type=MESH)
        return carry

    lax.fori_loop(1, NSEQ, greet, 0)
    pl.semaphore_signal(barrier, inc=1, device_id=((z + 1) % NZ, s), device_id_type=MESH)
    pl.semaphore_signal(barrier, inc=1, device_id=((z + NZ - 1) % NZ, s), device_id_type=MESH)

    @pl.when(zg != z)
    def _():
        for i in range(4):
            pl.semaphore_signal(barrier, inc=1, device_id=(zg, 4 * z + i), device_id_type=MESH)

    pl.semaphore_wait(barrier, jnp.where(zg != z, NSEQ - 1 + 2 + 4, NSEQ - 1 + 2))

    def slot(cc, uu, vv):
        uu = uu % NX
        vv = vv % NX
        yy = uu * (1 - cc) + vv * cc
        xx = vv * (1 - cc) + uu * cc
        return (yy * NX + xx) * 2 + cc

    class Gather:
        def __init__(self, buf, rows, send, recv_sem):
            self.buf, self.rows, self.send, self.recv = buf, rows, send, recv_sem

        def copy(self, sl, part, dev, sem):
            rows = self.rows
            if part is None:
                ref = self.buf.at[pl.ds(pl.multiple_of(sl * rows, rows), rows)]
            else:
                half = rows // 2
                ref = self.buf.at[pl.ds(pl.multiple_of(sl * rows + part * half, half), half)]
            return pltpu.make_async_remote_copy(
                src_ref=ref, dst_ref=ref, send_sem=self.send.at[sem], recv_sem=self.recv.at[sem],
                device_id=(z, dev), device_id_type=MESH,
            )

        def v_copy(self, k, recv_side=False):
            if k == 0:
                sl = slot(c, u, v - 1 if recv_side else v)
                return self.copy(sl, None, slot(c, u, v + 1), 0)
            if k == 1:
                sl = slot(c, u, v + 1 if recv_side else v)
                return self.copy(sl, None, slot(c, u, v - 1), 1)
            if k == 2:
                sl = slot(c, u, v - 2 if recv_side else v - 1)
                return self.copy(sl, 0, slot(c, u, v + 1), 2)
            sl = slot(c, u, v + 2 if recv_side else v + 1)
            return self.copy(sl, 1, slot(c, u, v - 1), 3)

        def u_copy(self, j, k, recv_side=False):
            vv = v + (0, -1, 1, 2)[j]
            sem = 4 + 4 * j + k
            if k == 0:
                sl = slot(c, u - 1 if recv_side else u, vv)
                return self.copy(sl, None, slot(c, u + 1, v), sem)
            if k == 1:
                sl = slot(c, u + 1 if recv_side else u, vv)
                return self.copy(sl, None, slot(c, u - 1, v), sem)
            if k == 2:
                sl = slot(c, u - 2 if recv_side else u - 1, vv)
                return self.copy(sl, 0, slot(c, u + 1, v), sem)
            sl = slot(c, u + 2 if recv_side else u + 1, vv)
            return self.copy(sl, 1, slot(c, u - 1, v), sem)

        def c_copy(self, a, j, recv_side=False):
            du = (0, -1, 1, 2)[a]
            dv = (0, -1, 1, 2)[j]
            if recv_side:
                sl = slot(1 - c, v + du, u + dv)
            else:
                sl = slot(c, u + du, v + dv)
            return self.copy(sl, None, s + 1 - 2 * c, 20 + 4 * a + j)

        def steps(self):
            def first():
                self.v_copy(0).start()
                self.v_copy(1).start()
                self.u_copy(0, 0).start()
                self.u_copy(0, 1).start()
                self.c_copy(0, 0).start()

            def second():
                self.v_copy(0, True).wait_recv()
                self.v_copy(2).start()
                self.v_copy(1, True).wait_recv()
                self.v_copy(3).start()
                for j in (1, 2):
                    self.u_copy(j, 0).start()
                    self.u_copy(j, 1).start()
                    self.c_copy(0, j).start()

            def third():
                self.v_copy(2, True).wait_recv()
                self.v_copy(3, True).wait_recv()
                self.u_copy(3, 0).start()
                self.u_copy(3, 1).start()
                self.c_copy(0, 3).start()

            def along(j):
                def run():
                    self.u_copy(j, 0, True).wait_recv()
                    self.u_copy(j, 2).start()
                    self.c_copy(1, j).start()
                    self.u_copy(j, 1, True).wait_recv()
                    self.u_copy(j, 3).start()
                    self.c_copy(2, j).start()
                return run

            def far(j):
                def run():
                    self.u_copy(j, 2, True).wait_recv()
                    self.u_copy(j, 3, True).wait_recv()
                    self.c_copy(3, j).start()
                return run

            def last():
                for a in range(4):
                    for j in range(4):
                        self.c_copy(a, j, True).wait_recv()

            return [
                first, second, along(0), third, along(1), along(2), far(0), along(3),
                far(1), far(2), far(3), last,
            ]

        def drain(self):
            for k in range(4):
                self.v_copy(k).wait_send()
            for j in range(4):
                for k in range(4):
                    self.u_copy(j, k).wait_send()
            for a in range(4):
                for j in range(4):
                    self.c_copy(a, j).wait_send()

    gather_w = Gather(wbuf, WROWS, w_send, w_recv)
    gather_o = Gather(obuf, OROWS, o_send, o_recv)
    w_steps = gather_w.steps()
    o_steps = gather_o.steps()
    w_steps[0]()

    own_o = pl.multiple_of(s * OROWS, OROWS)

    def scatter(i):
        return pltpu.make_async_remote_copy(
            src_ref=wo_ref.at[pl.ds(i * OROWS, OROWS)],
            dst_ref=obuf.at[pl.ds(pl.multiple_of((4 * z + i) * OROWS, OROWS), OROWS),
                            pl.ds(pl.multiple_of((s % 4) * 128, 128), 128)],
            send_sem=sc_send.at[i], recv_sem=sc_recv.at[s % 4],
            device_id=(zg, 4 * z + i), device_id_type=MESH,
        )

    def scattered(j):
        return pltpu.make_async_remote_copy(
            src_ref=wo_ref.at[pl.ds(j * OROWS, OROWS)],
            dst_ref=obuf.at[pl.ds(own_o, OROWS), pl.ds(j * 128, 128)],
            send_sem=sc_send.at[j], recv_sem=sc_recv.at[j],
            device_id=(zg, 4 * z + j), device_id_type=MESH,
        )

    for i in range(4):
        is_self = (zg == z) & (s % 4 == i)

        @pl.when(jnp.logical_not(is_self))
        def _(i=i):
            scatter(i).start()

        @pl.when(is_self)
        def _(i=i):
            cp = pltpu.make_async_copy(
                wo_ref.at[pl.ds(i * OROWS, OROWS)],
                obuf.at[pl.ds(own_o, OROWS), pl.ds(i * 128, 128)],
                loc_sem,
            )
            cp.start()
            cp.wait()

    def scales(t):
        pltpu.make_async_copy(
            tok_hbm.at[pl.ds(t * TILE, TILE)], tok.at[pl.ds(t * TILE, TILE)], tok_sem.at[t]
        ).wait()

        def rows(i, carry):
            at = pl.ds(pl.multiple_of(t * TILE + i * 16, 16), 16)
            val = tok[at, :].astype(F32)
            mean = jnp.sum(val * val, axis=-1, keepdims=True) * (1.0 / tok.shape[1])
            rscale[at, :] = jnp.broadcast_to(lax.rsqrt(mean + 1e-5), (16, 128))
            return carry

        lax.fori_loop(0, TILE // 16, rows, 0)

    def tables(h):
        def per_offset(d, carry):
            dy, dx = d // NX, d % NX
            src = (((y + NX - dy) % NX) * NX + (x + NX - dx) % NX) * 2 + (c + h) % 2
            dst = (((y + dy) % NX) * NX + (x + dx) % NX) * 2 + (c + h) % 2
            lab = jnp.int32(-1)
            til = jnp.int32(0)
            inv = jnp.int32(0)
            for t in range(TILES):
                code = codes_ref[src, h * TILES + t]
                hit = (code // 16) == s
                lab = jnp.where(hit, code % 16, lab)
                til = jnp.where(hit, t, til)
                mine = codes_ref[s, h * TILES + t]
                inv = jnp.where((mine // 16) == dst, t, inv)
            t_lab[h, d] = lab
            t_tile[h, d] = src * TILES + til
            t_inv[h, d] = inv
            return carry

        lax.fori_loop(0, NCHIP, per_offset, 0)

        def per_arrival(d, carry):
            lab = t_lab[h, d]
            want = jnp.where(lab < 0, -2, lab + 1 - 2 * (lab % 2))
            til = t_tile[h, d]
            par = d
            lim = jnp.int32(TILE)
            for e in range(NCHIP):
                hit = t_lab[h, e] == want
                par = jnp.where(hit, e, par)
                lim = jnp.where(hit & (t_tile[h, e] < til), 2 * TILE, lim)
            t_par[h, d] = par
            t_lim[h, d] = lim
            return carry

        lax.fori_loop(0, NCHIP, per_arrival, 0)
        for t in range(TILES):
            owner = codes_ref[s, h * TILES + t] // 32
            oy, ox = owner // NX, owner % NX
            t_dst[h, t] = ((oy + NX - y) % NX) * NX + (ox + NX - x) % NX

    work = [functools.partial(scales, t) for t in range(TILES)]
    work += [functools.partial(tables, h) for h in range(2)]
    order = list(w_steps[1:])
    while order or work:
        if work:
            work.pop(0)()
        if order and (len(order) > 1 or not work):
            order.pop(0)()

    def project(h):
        def rows(m, carry):
            at = pl.ds(pl.multiple_of(m * 256, 256), 256)
            val = jnp.dot(tok[at, :], wbuf[:, h * QKV:(h + 1) * QKV], preferred_element_type=F32)
            rs = rscale[at, :]
            parts = []
            for p in range(3):
                vp = (val[:, p * HW:(p + 1) * HW] * rs).astype(BF16)
                if p < 2:
                    vf = vp.astype(F32)
                    mean = jnp.mean(vf * vf, axis=-1, keepdims=True)
                    unit = vf * lax.rsqrt(mean + 1e-6)
                    if p == 0:
                        unit = unit * (LOGIT * LOG2E)
                    vp = unit.astype(BF16)
                parts.append(vp)
            whole = jnp.concatenate(parts, axis=1)
            qkv[h][pl.ds(m * 2, 2)] = whole.reshape(2, TILE, QKV)
            return carry

        lax.fori_loop(0, TILES // 2, rows, 0)

    def a_copy(h, d, recv_side=False):
        dy, dx = d // NX, d % NX
        dev = (((y + dy) % NX) * NX + (x + dx) % NX) * 2 + (c + h) % 2
        return pltpu.make_async_remote_copy(
            src_ref=stage[h].at[d], dst_ref=recv[h].at[d],
            send_sem=a_send.at[h, d], recv_sem=a_recv.at[h, d],
            device_id=(z, dev), device_id_type=MESH,
        )

    def r_copy(h, d):
        dy, dx = d // NX, d % NX
        dev = (((y + NX - dy) % NX) * NX + (x + NX - dx) % NX) * 2 + (c + h) % 2
        return pltpu.make_async_remote_copy(
            src_ref=ret[h].at[d], dst_ref=back[h].at[d],
            send_sem=r_send.at[h, d], recv_sem=r_recv.at[h, d],
            device_id=(z, dev), device_id_type=MESH,
        )

    def send_tiles(h):
        if h == 0:
            recv[0][0] = qkv[0][t_inv[0, 0]]

        def one(d, carry):
            stage[h][d] = qkv[h][t_inv[h, d]]
            a_copy(h, d).start()
            return carry

        lax.fori_loop(1 - h, NCHIP, one, 0)

    def arrivals(h):
        def one(d, carry):
            a_copy(h, d).wait_recv()
            return carry

        lax.fori_loop(1 - h, NCHIP, one, 0)

    def attend(h):
        row = lax.broadcasted_iota(jnp.int32, (TILE, 2 * TILE), 0)
        col = lax.broadcasted_iota(jnp.int32, (TILE, 2 * TILE), 1)
        ones = jnp.ones((2 * TILE, HW), BF16)

        def one(d, store):
            par = t_par[h, d]
            lim = t_lim[h, d]
            mine = recv[h][d]
            other = recv[h][par]
            keys = jnp.concatenate([mine[:, HW:2 * HW], other[:, HW:2 * HW]], axis=0)
            vals = jnp.concatenate([mine[:, 2 * HW:], other[:, 2 * HW:]], axis=0)
            logits = lax.dot_general(
                mine[:, :HW], keys, (((1,), (1,)), ((), ())), preferred_element_type=F32
            )
            allowed = (col <= row) | ((col >= TILE) & (col < lim))
            probs = jnp.where(allowed, jnp.exp2(logits), 0.0).astype(BF16)
            both = jnp.dot(
                probs, jnp.concatenate([vals, ones], axis=1), preferred_element_type=F32
            )
            store[h][d] = (both[:, :HW] / both[:, HW:]).astype(BF16)
            ksum[h, d] = jnp.sum(mine[:, HW:2 * HW].astype(F32).reshape(16, 8, HW), axis=0)

        if h == 0:
            one(0, back)

        def loop(d, carry):
            one(d, ret)
            r_copy(h, d).start()
            return carry

        lax.fori_loop(1 - h, NCHIP, loop, 0)

    def centroids(h):
        rows8 = lax.broadcasted_iota(jnp.int32, (8, HW), 0)

        def one(d, carry):
            sums, counts = carry
            cl = (t_lab[h, d] + 2) // 2 - 1
            hit = rows8 == cl
            tot = jnp.sum(ksum[h, d], axis=0, keepdims=True)
            sums = sums + jnp.where(hit, jnp.broadcast_to(tot, (8, HW)), 0.0)
            counts = counts + jnp.where(hit, float(TILE), 0.0)
            return sums, counts

        zero = jnp.zeros((8, HW), F32)
        sums, counts = lax.fori_loop(0, NCHIP, one, (zero, zero))
        cent = cent_ref[h]
        means = sums / jnp.maximum(counts, 1.0)
        newc_ref[h] = cent + 0.25 * jnp.where(counts > 0, means - cent, 0.0)

    def come_home(h):
        def one(d, carry):
            r_copy(h, d).wait_recv()
            return carry

        lax.fori_loop(1 - h, NCHIP, one, 0)
        for t in range(TILES):
            gbuf[h, z, pl.ds(t * TILE, TILE)] = back[h][t_dst[h, t]]

    half = TILES * TILE // 2

    def z_copy(h, way, k, j, recv_side=False):
        sign = 1 if way == 0 else -1
        at = z - sign * (k - 1)
        if recv_side:
            at = at - sign
        ref = gbuf.at[h, (at + 2 * NZ) % NZ, pl.ds(j * half, half)]
        idx = way * 8 + (k - 1) * 2 + j
        return pltpu.make_async_remote_copy(
            src_ref=ref, dst_ref=ref, send_sem=z_send.at[h, idx], recv_sem=z_recv.at[h, idx],
            device_id=((z + sign + NZ) % NZ, s), device_id_type=MESH,
        )

    def z_parts(k):
        if k < 4:
            return [(way, j) for j in range(2) for way in range(2)]
        return [(0, 0), (1, 1)]

    def z_first(h):
        for way, j in z_parts(1):
            z_copy(h, way, 1, j).start()

    def z_step(h, k):
        nxt = z_parts(k + 1) if k < 4 else []
        for way, j in z_parts(k):
            z_copy(h, way, k, j, True).wait_recv()
            if (way, j) in nxt:
                z_copy(h, way, k + 1, j).start()

    def z_drain(h):
        for k in range(1, 5):
            for way, j in z_parts(k):
                z_copy(h, way, k, j).wait_send()

    def multiply(h, ga, gb, mode):
        ga = (z + ga) % NZ
        gb = (z + gb) % NZ

        def cols(n, carry):
            at = pl.ds(pl.multiple_of(n * 256, 256), 256)
            rhs = jnp.concatenate([gbuf[h, ga, at], gbuf[h, gb, at]], axis=1)
            lhs = jnp.concatenate([owt[h, ga], owt[h, gb]], axis=1)
            val = lax.dot_general(lhs, rhs, (((1,), (1,)), ((), ())), preferred_element_type=F32)
            if mode != "first":
                val = val + acc[n]
            if mode == "last":
                for m in range(4):
                    @pl.when(n == m)
                    def _(m=m):
                        out_ref[:, m * 256:(m + 1) * 256] = val.astype(BF16)
            else:
                acc[n] = val
            return carry

        lax.fori_loop(0, 4, cols, 0)

    project(0)
    send_tiles(0)
    project(1)
    send_tiles(1)
    arrivals(0)
    attend(0)
    come_home(0)
    z_first(0)
    arrivals(1)
    z_step(0, 1)
    attend(1)
    centroids(0)
    for j in range(4):
        not_self = (zg != z) | (s % 4 != j)

        @pl.when(not_self)
        def _(j=j):
            scattered(j).wait_recv()

    o_steps[0]()
    z_step(0, 2)
    o_steps[1]()
    come_home(1)
    z_first(1)
    centroids(1)
    z_step(0, 3)
    for f in o_steps[2:]:
        f()
    for g in range(NZ):
        for h in range(2):
            at = (g * 2 + h) * HW
            owt[h, g] = obuf[at:at + HW, :].astype(F32).T.astype(BF16)
    z_step(1, 1)
    z_step(0, 4)
    multiply(0, 0, 1, "first")
    multiply(0, 7, 2, "mid")
    z_step(1, 2)
    multiply(0, 6, 3, "mid")
    multiply(0, 5, 4, "mid")
    multiply(1, 1, 7, "mid")
    z_step(1, 3)
    multiply(1, 2, 6, "mid")
    multiply(1, 3, 5, "mid")
    z_step(1, 4)
    multiply(1, 0, 4, "last")

    gather_w.drain()
    gather_o.drain()
    for i in range(4):
        @pl.when((zg != z) | (s % 4 != i))
        def _(i=i):
            scatter(i).wait_send()

    for h in range(2):
        def sent(d, carry, h=h):
            a_copy(h, d).wait_send()
            r_copy(h, d).wait_send()
            return carry

        lax.fori_loop(1 - h, NCHIP, sent, 0)
        z_drain(h)


def on_device(tokens, qkv_weight, out_weight, centroids, clusters, slots):
    codes = lax.all_gather(clusters * 2 + slots, "seq", axis=0, tiled=False).reshape(NSEQ, 16)
    vmem = pl.BlockSpec(memory_space=pltpu.VMEM)
    dma = pltpu.SemaphoreType.DMA
    return pl.pallas_call(
        kernel,
        out_shape=(
            jax.ShapeDtypeStruct((OCOLS, TILES * TILE), BF16),
            jax.ShapeDtypeStruct(centroids.shape, F32),
        ),
        in_specs=[
            pl.BlockSpec(memory_space=pltpu.SMEM),
            pl.BlockSpec(memory_space=pl.ANY),
            vmem, vmem, vmem,
        ],
        out_specs=(vmem, vmem),
        scratch_shapes=[
            pltpu.VMEM(tokens.shape, BF16),
            pltpu.VMEM((NSEQ * WROWS, 2 * QKV), BF16),
            pltpu.VMEM((NSEQ * OROWS, OCOLS), BF16),
            pltpu.VMEM((2, NZ, OCOLS, HW), BF16),
            pltpu.VMEM((TILES * TILE, 128), F32),
        ]
        + [pltpu.VMEM((TILES, TILE, QKV), BF16)] * 2
        + [pltpu.VMEM((NCHIP, TILE, QKV), BF16)] * 4
        + [pltpu.VMEM((NCHIP, TILE, HW), BF16)] * 4
        + [
            pltpu.VMEM((2, NZ, TILES * TILE, HW), BF16),
            pltpu.VMEM((4, OCOLS, 256), F32),
            pltpu.VMEM((2, NCHIP, 8, HW), F32),
        ]
        + [pltpu.SMEM((2, NCHIP), jnp.int32)] * 5
        + [pltpu.SMEM((2, TILES), jnp.int32)]
        + [
            dma((TILES,)), dma((36,)), dma((36,)), dma((36,)), dma((36,)),
            dma((4,)), dma((4,)), dma,
            dma((2, NCHIP)), dma((2, NCHIP)), dma((2, NCHIP)), dma((2, NCHIP)),
            dma((2, 16)), dma((2, 16)),
        ],
        compiler_params=pltpu.CompilerParams(
            collective_id=0, has_side_effects=True, vmem_limit_bytes=60 * 1024 * 1024
        ),
    )(codes, tokens, qkv_weight, out_weight, centroids)


def solution(mesh):
    return jax.shard_map(
        on_device,
        mesh=mesh,
        in_specs=(
            P("seq", None),
            P("seq", "head"),
            P("head", "seq"),
            P("head", "seq", None),
            P("head", "seq"),
            P("head", "seq"),
        ),
        out_specs=(P("head", "seq"), P("head", "seq", None)),
        check_vma=False,
    )
```

```python
import functools

import jax
import jax.numpy as jnp
from jax import lax
from jax.experimental import pallas as pl
from jax.experimental.pallas import tpu as pltpu
from jax.sharding import PartitionSpec as P

MESH = pl.DeviceIdType.MESH
F32 = jnp.float32
BF16 = jnp.bfloat16

NX = 4
NZ = 8
NCHIP = 16
NSEQ = 32
TILE = 128
TILES = 8
HW = 128
QKV = 3 * HW
WROWS = 128
OROWS = 64
OCOLS = 512
MROWS = TILE + 8
LOG2E = 1.4426950408889634
LOGIT = 8.0 / 128


def kernel(
    clus_ref, slot_ref, tok_hbm, w_ref, wo_ref, cent_ref,
    out_ref, newc_ref,
    tok, wbuf, obuf, owt, rscale,
    qkv0, qkv1, stage0, stage1, recv0, recv1, ret0, ret1, back0, back1,
    gbuf, acc, msg0, msg1, own0, own1, late,
    codes_ref, cbuf, t_inv, t_lab, t_tile, t_par, t_lim, t_dst,
    tok_sem, w_send, w_recv, o_send, o_recv, sc_send, sc_recv, loc_sem,
    a_send, a_recv, r_send, r_recv, z_send, z_recv, m_send, m_recv,
):
    z = lax.axis_index("head")
    s = lax.axis_index("seq")
    c = s % 2
    q = s // 2
    x = q % NX
    y = q // NX
    u = y * (1 - c) + x * c
    v = x * (1 - c) + y * c
    qkv = (qkv0, qkv1)
    stage = (stage0, stage1)
    recv = (recv0, recv1)
    ret = (ret0, ret1)
    back = (back0, back1)
    msg = (msg0, msg1)
    own = (own0, own1)

    for t in range(TILES):
        pltpu.make_async_copy(
            tok_hbm.at[pl.ds(t * TILE, TILE)], tok.at[pl.ds(t * TILE, TILE)], tok_sem.at[t]
        ).start()
    own_w = pl.ds(pl.multiple_of(s * WROWS, WROWS), WROWS)
    wbuf[own_w, :] = w_ref[...]
    own_codes = clus_ref[...] * 2 + slot_ref[...]
    cbuf[s] = jnp.full((2, 128), -16, jnp.int32)
    cbuf[s, :, 0:TILES] = own_codes

    zg = s // 4
    barrier = pltpu.get_barrier_semaphore()

    def greet(i, carry):
        pl.semaphore_signal(barrier, inc=1, device_id=(z, (s + i) % NSEQ), device_id_type=MESH)
        return carry

    lax.fori_loop(1, NSEQ, greet, 0)
    pl.semaphore_signal(barrier, inc=1, device_id=((z + 1) % NZ, s), device_id_type=MESH)
    pl.semaphore_signal(barrier, inc=1, device_id=((z + NZ - 1) % NZ, s), device_id_type=MESH)

    @pl.when(zg != z)
    def _():
        for i in range(4):
            pl.semaphore_signal(barrier, inc=1, device_id=(zg, 4 * z + i), device_id_type=MESH)

    def scales(t):
        pltpu.make_async_copy(
            tok_hbm.at[pl.ds(t * TILE, TILE)], tok.at[pl.ds(t * TILE, TILE)], tok_sem.at[t]
        ).wait()

        def rows(i, carry):
            at = pl.ds(pl.multiple_of(t * TILE + i * 16, 16), 16)
            val = tok[at, :].astype(F32)
            mean = jnp.sum(val * val, axis=-1, keepdims=True) * (1.0 / tok.shape[1])
            rscale[at, :] = jnp.broadcast_to(lax.rsqrt(mean + 1e-5), (16, 128))
            return carry

        lax.fori_loop(0, TILE // 16, rows, 0)

    pl.semaphore_wait(barrier, jnp.where(zg != z, NSEQ - 1 + 2 + 4, NSEQ - 1 + 2))

    def slot(cc, uu, vv):
        uu = uu % NX
        vv = vv % NX
        yy = uu * (1 - cc) + vv * cc
        xx = vv * (1 - cc) + uu * cc
        return (yy * NX + xx) * 2 + cc

    class Gather:
        def __init__(self, buf, rows, send, recv_sem, cols=None):
            self.buf, self.rows, self.send, self.recv = buf, rows, send, recv_sem
            self.cols = slice(None) if cols is None else pl.ds(*cols)

        def copy(self, sl, part, dev, sem):
            rows = self.rows
            if part is None:
                ref = self.buf.at[pl.ds(pl.multiple_of(sl * rows, rows), rows), self.cols]
            else:
                half = rows // 2
                ref = self.buf.at[pl.ds(pl.multiple_of(sl * rows + part * half, half), half), self.cols]
            return pltpu.make_async_remote_copy(
                src_ref=ref, dst_ref=ref, send_sem=self.send.at[sem], recv_sem=self.recv.at[sem],
                device_id=(z, dev), device_id_type=MESH,
            )

        def v_copy(self, k, recv_side=False):
            if k == 0:
                sl = slot(c, u, v - 1 if recv_side else v)
                return self.copy(sl, None, slot(c, u, v + 1), 0)
            if k == 1:
                sl = slot(c, u, v + 1 if recv_side else v)
                return self.copy(sl, None, slot(c, u, v - 1), 1)
            if k == 2:
                sl = slot(c, u, v - 2 if recv_side else v - 1)
                return self.copy(sl, 0, slot(c, u, v + 1), 2)
            sl = slot(c, u, v + 2 if recv_side else v + 1)
            return self.copy(sl, 1, slot(c, u, v - 1), 3)

        def u_copy(self, j, k, recv_side=False):
            vv = v + (0, -1, 1, 2)[j]
            sem = 4 + 4 * j + k
            if k == 0:
                sl = slot(c, u - 1 if recv_side else u, vv)
                return self.copy(sl, None, slot(c, u + 1, v), sem)
            if k == 1:
                sl = slot(c, u + 1 if recv_side else u, vv)
                return self.copy(sl, None, slot(c, u - 1, v), sem)
            if k == 2:
                sl = slot(c, u - 2 if recv_side else u - 1, vv)
                return self.copy(sl, 0, slot(c, u + 1, v), sem)
            sl = slot(c, u + 2 if recv_side else u + 1, vv)
            return self.copy(sl, 1, slot(c, u - 1, v), sem)

        def c_copy(self, a, j, recv_side=False):
            du = (0, -1, 1, 2)[a]
            dv = (0, -1, 1, 2)[j]
            if recv_side:
                sl = slot(1 - c, v + du, u + dv)
            else:
                sl = slot(c, u + du, v + dv)
            return self.copy(sl, None, s + 1 - 2 * c, 20 + 4 * a + j)

        def steps(self):
            def first():
                self.v_copy(0).start()
                self.v_copy(1).start()
                self.u_copy(0, 0).start()
                self.u_copy(0, 1).start()
                self.c_copy(0, 0).start()

            def second():
                self.v_copy(0, True).wait_recv()
                self.v_copy(2).start()
                self.v_copy(1, True).wait_recv()
                self.v_copy(3).start()
                for j in (1, 2):
                    self.u_copy(j, 0).start()
                    self.u_copy(j, 1).start()
                    self.c_copy(0, j).start()

            def third():
                self.v_copy(2, True).wait_recv()
                self.v_copy(3, True).wait_recv()
                self.u_copy(3, 0).start()
                self.u_copy(3, 1).start()
                self.c_copy(0, 3).start()

            def along(j):
                def run():
                    self.u_copy(j, 0, True).wait_recv()
                    self.u_copy(j, 2).start()
                    self.c_copy(1, j).start()
                    self.u_copy(j, 1, True).wait_recv()
                    self.u_copy(j, 3).start()
                    self.c_copy(2, j).start()
                return run

            def far(j):
                def run():
                    self.u_copy(j, 2, True).wait_recv()
                    self.u_copy(j, 3, True).wait_recv()
                    self.c_copy(3, j).start()
                return run

            def last():
                for a in range(4):
                    for j in range(4):
                        self.c_copy(a, j, True).wait_recv()

            return [
                first, second, along(0), third, along(1), along(2), far(0), along(3),
                far(1), far(2), far(3), last,
            ]

        def drain(self):
            for k in range(4):
                self.v_copy(k).wait_send()
            for j in range(4):
                for k in range(4):
                    self.u_copy(j, k).wait_send()
            for a in range(4):
                for j in range(4):
                    self.c_copy(a, j).wait_send()

    gather_w = [
        Gather(wbuf, WROWS, w_send.at[h], w_recv.at[h], (h * QKV, QKV)) for h in range(2)
    ]
    gather_o = Gather(obuf, OROWS, o_send, o_recv)
    w_steps = [g.steps() for g in gather_w]
    o_steps = gather_o.steps()
    w_steps[0][0]()
    w_steps[1][0]()

    def code_copy(i, recv_side=False):
        at = (s + NSEQ - i) % NSEQ if recv_side else s
        return pltpu.make_async_remote_copy(
            src_ref=cbuf.at[at], dst_ref=cbuf.at[at], send_sem=m_send.at[i], recv_sem=m_recv.at[i],
            device_id=(z, (s + i) % NSEQ), device_id_type=MESH,
        )

    def send_codes(i, carry):
        code_copy(i).start()
        return carry

    lax.fori_loop(1, NSEQ, send_codes, 0)

    def codes_here():
        def one(i, carry):
            code_copy(i, True).wait_recv()
            return carry

        lax.fori_loop(1, NSEQ, one, 0)
        pltpu.make_async_copy(cbuf, codes_ref, loc_sem).start()

    def codes_read():
        pltpu.make_async_copy(cbuf, codes_ref, loc_sem).wait()

    def lateness():
        place = lax.broadcasted_iota(jnp.int32, (NSEQ, 128), 0) * TILES
        place = place + lax.broadcasted_iota(jnp.int32, (NSEQ, 128), 1)
        for h in range(2):
            codes = cbuf[:, h, :]
            for t in range(TILES):
                mine = own_codes[h:h + 1, t:t + 1]
                want = jnp.broadcast_to(mine + 1 - 2 * (mine % 2), (NSEQ, 128))
                hit = (codes == want) & (place < s * TILES + t)
                some = jnp.max(jnp.where(hit, 1, 0), axis=0, keepdims=True)
                some = jnp.max(some, axis=1, keepdims=True)
                late[h * TILES + t:h * TILES + t + 1, :] = jnp.broadcast_to(some, (1, 128))

    own_o = pl.multiple_of(s * OROWS, OROWS)

    def scatter(i):
        return pltpu.make_async_remote_copy(
            src_ref=wo_ref.at[pl.ds(i * OROWS, OROWS)],
            dst_ref=obuf.at[pl.ds(pl.multiple_of((4 * z + i) * OROWS, OROWS), OROWS),
                            pl.ds(pl.multiple_of((s % 4) * 128, 128), 128)],
            send_sem=sc_send.at[i], recv_sem=sc_recv.at[s % 4],
            device_id=(zg, 4 * z + i), device_id_type=MESH,
        )

    def scattered(j):
        return pltpu.make_async_remote_copy(
            src_ref=wo_ref.at[pl.ds(j * OROWS, OROWS)],
            dst_ref=obuf.at[pl.ds(own_o, OROWS), pl.ds(j * 128, 128)],
            send_sem=sc_send.at[j], recv_sem=sc_recv.at[j],
            device_id=(zg, 4 * z + j), device_id_type=MESH,
        )

    for i in range(4):
        is_self = (zg == z) & (s % 4 == i)

        @pl.when(jnp.logical_not(is_self))
        def _(i=i):
            scatter(i).start()

        @pl.when(is_self)
        def _(i=i):
            cp = pltpu.make_async_copy(
                wo_ref.at[pl.ds(i * OROWS, OROWS)],
                obuf.at[pl.ds(own_o, OROWS), pl.ds(i * 128, 128)],
                loc_sem,
            )
            cp.start()
            cp.wait()

    def tables(h):
        def per_offset(d, carry):
            dy, dx = d // NX, d % NX
            src = (((y + NX - dy) % NX) * NX + (x + NX - dx) % NX) * 2 + (c + h) % 2
            dst = (((y + dy) % NX) * NX + (x + dx) % NX) * 2 + (c + h) % 2
            lab = jnp.int32(-1)
            til = jnp.int32(0)
            inv = jnp.int32(0)
            for t in range(TILES):
                code = codes_ref[src, h, t]
                hit = (code // 16) == s
                lab = jnp.where(hit, code % 16, lab)
                til = jnp.where(hit, t, til)
                mine = codes_ref[s, h, t]
                inv = jnp.where((mine // 16) == dst, t, inv)
            t_lab[h, d] = lab
            t_tile[h, d] = src * TILES + til
            t_inv[h, d] = inv
            return carry

        lax.fori_loop(0, NCHIP, per_offset, 0)

        def per_arrival(d, carry):
            lab = t_lab[h, d]
            want = jnp.where(lab < 0, -2, lab + 1 - 2 * (lab % 2))
            til = t_tile[h, d]
            par = d
            lim = jnp.int32(TILE)
            for e in range(NCHIP):
                hit = t_lab[h, e] == want
                par = jnp.where(hit, e, par)
                lim = jnp.where(hit & (t_tile[h, e] < til), 2 * TILE, lim)
            t_par[h, d] = par
            t_lim[h, d] = lim
            return carry

        lax.fori_loop(0, NCHIP, per_arrival, 0)
        for t in range(TILES):
            owner = codes_ref[s, h, t] // 32
            oy, ox = owner // NX, owner % NX
            t_dst[h, t] = ((oy + NX - y) % NX) * NX + (ox + NX - x) % NX

    lag = 4
    for k in range(1, 12):
        w_steps[0][k]()
        if k <= TILES:
            scales(k - 1)
        if k - lag >= 1:
            w_steps[1][k - lag]()
        if k == 5:
            codes_here()
            lateness()
        if k == 8:
            codes_read()
        if k in (8, 9):
            tables(k - 8)

    def project(h, m):
        if True:
            at = pl.ds(pl.multiple_of(m * 256, 256), 256)
            val = jnp.dot(tok[at, :], wbuf[:, h * QKV:(h + 1) * QKV], preferred_element_type=F32)
            rs = rscale[at, :]
            unit = []
            for p in range(2):
                vf = (val[:, p * HW:(p + 1) * HW] * rs).astype(BF16).astype(F32)
                mean = jnp.mean(vf * vf, axis=-1, keepdims=True)
                unit.append(vf * lax.rsqrt(mean + 1e-6))
            query = (unit[0] * (LOGIT * LOG2E)).astype(BF16)
            key = unit[1].astype(BF16)
            value = (val[:, 2 * HW:] * rs).astype(BF16)
            row8 = lax.broadcasted_iota(jnp.int32, (8, HW), 0)
            for i in range(2):
                t = m * 2 + i
                part = slice(i * TILE, (i + 1) * TILE)
                qkv[h][t, :, :HW] = query[part]
                qkv[h][t, :, HW:2 * HW] = key[part]
                qkv[h][t, :, 2 * HW:] = value[part]
                is_late = jnp.broadcast_to(late[h * TILES + t:h * TILES + t + 1, :], (TILE, HW)) > 0
                msg[h][t, :TILE, :HW] = jnp.where(is_late, query[part], key[part])
                msg[h][t, :TILE, HW:] = value[part]
                tot = jnp.sum(unit[1][part], axis=0, keepdims=True)
                high = tot.astype(BF16).astype(F32)
                extra = jnp.where(row8 == 0, high, jnp.where(row8 == 1, tot - high, 0.0))
                msg[h][t, TILE:, :HW] = extra.astype(BF16)
                msg[h][t, TILE:, HW:] = jnp.zeros((8, HW), BF16)

    def a_copy(h, d, recv_side=False):
        dy, dx = d // NX, d % NX
        dev = (((y + dy) % NX) * NX + (x + dx) % NX) * 2 + (c + h) % 2
        return pltpu.make_async_remote_copy(
            src_ref=stage[h].at[d], dst_ref=recv[h].at[d],
            send_sem=a_send.at[h, d], recv_sem=a_recv.at[h, d],
            device_id=(z, dev), device_id_type=MESH,
        )

    def r_copy(h, d):
        dy, dx = d // NX, d % NX
        dev = (((y + NX - dy) % NX) * NX + (x + NX - dx) % NX) * 2 + (c + h) % 2
        return pltpu.make_async_remote_copy(
            src_ref=ret[h].at[d], dst_ref=back[h].at[d],
            send_sem=r_send.at[h, d], recv_sem=r_recv.at[h, d],
            device_id=(z, dev), device_id_type=MESH,
        )

    def stage_tiles(h):
        if h == 0:
            recv[0][0] = msg[0][t_inv[0, 0]]

        def one(d, carry):
            stage[h][d] = msg[h][t_inv[h, d]]
            return carry

        lax.fori_loop(1 - h, NCHIP, one, 0)

    def send_tiles(h):
        def one(d, carry):
            a_copy(h, d).start()
            return carry

        lax.fori_loop(1 - h, NCHIP, one, 0)

    def arrivals(h):
        def one(d, carry):
            a_copy(h, d).wait_recv()
            return carry

        lax.fori_loop(1 - h, NCHIP, one, 0)

    row = lax.broadcasted_iota(jnp.int32, (TILE, TILE), 0)
    col = lax.broadcasted_iota(jnp.int32, (TILE, TILE), 1)
    ones = jnp.ones((TILE, HW), BF16)
    contract_last = (((1,), (1,)), ((), ()))

    def attend_own(h):
        def one(t, carry):
            mine = qkv[h][t]
            logits = lax.dot_general(
                mine[:, :HW], mine[:, HW:2 * HW], contract_last, preferred_element_type=F32
            )
            probs = jnp.where(col <= row, jnp.exp2(logits), 0.0).astype(BF16)
            own[h][t] = jnp.dot(
                probs, jnp.concatenate([mine[:, 2 * HW:], ones], axis=1),
                preferred_element_type=F32,
            )
            return carry

        lax.fori_loop(0, TILES, one, 0)

    def attend(h):
        row8 = lax.broadcasted_iota(jnp.int32, (8, TILE), 0)
        ones8 = jnp.ones((8, TILE), BF16)

        def one(d, store):
            earlier = recv[h][t_par[h, d]]
            logits = lax.dot_general(
                recv[h][d, :TILE, :HW], earlier[:TILE, :HW], contract_last,
                preferred_element_type=F32,
            )
            logits = jnp.where(col < t_lim[h, d] - TILE, logits, 0.0)
            probs = jnp.exp2(logits).astype(BF16)
            both = jnp.dot(
                probs, jnp.concatenate([earlier[:TILE, HW:], ones], axis=1),
                preferred_element_type=F32,
            )
            tot = lax.dot_general(ones8, probs, contract_last, preferred_element_type=F32)
            high = tot.astype(BF16).astype(F32)
            extra = jnp.where(row8 == 0, high, jnp.where(row8 == 1, tot - high, 0.0))
            store[h][d, :TILE] = (both[:, :HW] / both[:, HW:]).astype(BF16)
            store[h][d, TILE:] = extra.astype(BF16)

        if h == 0:
            one(0, back)

        def loop(d, carry):
            one(d, ret)
            r_copy(h, d).start()
            return carry

        lax.fori_loop(1 - h, NCHIP, loop, 0)

    def centroids(h):
        rows8 = lax.broadcasted_iota(jnp.int32, (8, HW), 0)

        def one(d, carry):
            sums, counts = carry
            cl = (t_lab[h, d] + 2) // 2 - 1
            hit = rows8 == cl
            tot = jnp.sum(recv[h][d, TILE:, :HW].astype(F32), axis=0, keepdims=True)
            sums = sums + jnp.where(hit, jnp.broadcast_to(tot, (8, HW)), 0.0)
            counts = counts + jnp.where(hit, float(TILE), 0.0)
            return sums, counts

        zero = jnp.zeros((8, HW), F32)
        sums, counts = lax.fori_loop(0, NCHIP, one, (zero, zero))
        cent = cent_ref[h]
        means = sums / jnp.maximum(counts, 1.0)
        newc_ref[h] = cent + 0.25 * jnp.where(counts > 0, means - cent, 0.0)

    def come_home(h):
        def one(d, carry):
            r_copy(h, d).wait_recv()
            return carry

        lax.fori_loop(1 - h, NCHIP, one, 0)
        for t in range(TILES):
            far = back[h][t_dst[h, t]]
            is_late = jnp.broadcast_to(late[h * TILES + t:h * TILES + t + 1, :], (TILE, HW)) > 0
            weight = lax.dot_general(
                far[TILE:], jnp.ones((8, HW), BF16), (((0,), (0,)), ((), ())),
                preferred_element_type=F32,
            )
            top = own[h][t, :, :HW] + jnp.where(is_late, weight * far[:TILE].astype(F32), 0.0)
            low = own[h][t, :, HW:] + jnp.where(is_late, weight, 0.0)
            gbuf[h, z, pl.ds(t * TILE, TILE)] = (top / low).astype(BF16)

    half = TILES * TILE // 2

    def z_copy(h, way, k, j, recv_side=False):
        sign = 1 if way == 0 else -1
        at = z - sign * (k - 1)
        if recv_side:
            at = at - sign
        ref = gbuf.at[h, (at + 2 * NZ) % NZ, pl.ds(j * half, half)]
        idx = way * 8 + (k - 1) * 2 + j
        return pltpu.make_async_remote_copy(
            src_ref=ref, dst_ref=ref, send_sem=z_send.at[h, idx], recv_sem=z_recv.at[h, idx],
            device_id=((z + sign + NZ) % NZ, s), device_id_type=MESH,
        )

    def z_parts(k):
        if k < 4:
            return [(way, j) for j in range(2) for way in range(2)]
        return [(0, 0), (1, 1)]

    def z_first(h):
        for way, j in z_parts(1):
            z_copy(h, way, 1, j).start()

    def z_step(h, k):
        nxt = z_parts(k + 1) if k < 4 else []
        for way, j in z_parts(k):
            z_copy(h, way, k, j, True).wait_recv()
            if (way, j) in nxt:
                z_copy(h, way, k + 1, j).start()

    def z_drain(h):
        for k in range(1, 5):
            for way, j in z_parts(k):
                z_copy(h, way, k, j).wait_send()

    def multiply(h, ga, gb, mode):
        ga = (z + ga) % NZ
        gb = (z + gb) % NZ

        def cols(n, carry):
            at = pl.ds(pl.multiple_of(n * 256, 256), 256)
            rhs = jnp.concatenate([gbuf[h, ga, at], gbuf[h, gb, at]], axis=1)
            lhs = jnp.concatenate([owt[h, ga], owt[h, gb]], axis=1)
            val = lax.dot_general(lhs, rhs, (((1,), (1,)), ((), ())), preferred_element_type=F32)
            if mode != "first":
                val = val + acc[n]
            if mode == "last":
                for m in range(4):
                    @pl.when(n == m)
                    def _(m=m):
                        out_ref[:, m * 256:(m + 1) * 256] = val.astype(BF16)
            else:
                acc[n] = val
            return carry

        lax.fori_loop(0, 4, cols, 0)

    rest = w_steps[1][12 - lag:]
    for m in range(4):
        project(0, m)
        if m < 3 and rest:
            rest.pop(0)()
    stage_tiles(0)
    send_tiles(0)
    for f in rest:
        f()
    for m in range(4):
        project(1, m)
    stage_tiles(1)
    attend_own(0)
    attend_own(1)
    arrivals(0)
    attend(0)
    send_tiles(1)
    come_home(0)
    z_first(0)
    z_step(0, 1)
    z_step(0, 2)
    arrivals(1)
    attend(1)
    z_step(0, 3)
    centroids(0)
    for j in range(4):
        not_self = (zg != z) | (s % 4 != j)

        @pl.when(not_self)
        def _(j=j):
            scattered(j).wait_recv()

    o_steps[0]()
    o_steps[1]()
    come_home(1)
    z_first(1)
    centroids(1)
    o_steps[2]()
    o_steps[3]()
    o_steps[4]()
    o_steps[5]()
    z_step(1, 1)
    o_steps[6]()
    o_steps[7]()
    z_step(0, 4)
    o_steps[8]()
    o_steps[9]()
    z_step(1, 2)
    o_steps[10]()
    o_steps[11]()
    for g in range(NZ):
        for h in range(2):
            at = (g * 2 + h) * HW
            owt[h, g] = obuf[at:at + HW, :].astype(F32).T.astype(BF16)
    multiply(0, 0, 1, "first")
    multiply(0, 7, 2, "mid")
    z_step(1, 3)
    multiply(0, 6, 3, "mid")
    multiply(0, 5, 4, "mid")
    multiply(1, 1, 7, "mid")
    multiply(1, 2, 6, "mid")
    multiply(1, 3, 5, "mid")
    z_step(1, 4)
    multiply(1, 0, 4, "last")

    gather_w[0].drain()
    gather_w[1].drain()
    gather_o.drain()

    def codes_sent(i, carry):
        code_copy(i).wait_send()
        return carry

    lax.fori_loop(1, NSEQ, codes_sent, 0)
    for i in range(4):
        @pl.when((zg != z) | (s % 4 != i))
        def _(i=i):
            scatter(i).wait_send()

    for h in range(2):
        def sent(d, carry, h=h):
            a_copy(h, d).wait_send()
            r_copy(h, d).wait_send()
            return carry

        lax.fori_loop(1 - h, NCHIP, sent, 0)
        z_drain(h)


def on_device(tokens, qkv_weight, out_weight, centroids, clusters, slots):
    vmem = pl.BlockSpec(memory_space=pltpu.VMEM)
    dma = pltpu.SemaphoreType.DMA
    return pl.pallas_call(
        kernel,
        out_shape=(
            jax.ShapeDtypeStruct((OCOLS, TILES * TILE), BF16),
            jax.ShapeDtypeStruct(centroids.shape, F32),
        ),
        in_specs=[
            vmem, vmem,
            pl.BlockSpec(memory_space=pl.ANY),
            vmem, vmem, vmem,
        ],
        out_specs=(vmem, vmem),
        scratch_shapes=[
            pltpu.VMEM(tokens.shape, BF16),
            pltpu.VMEM((NSEQ * WROWS, 2 * QKV), BF16),
            pltpu.VMEM((NSEQ * OROWS, OCOLS), BF16),
            pltpu.VMEM((2, NZ, OCOLS, HW), BF16),
            pltpu.VMEM((TILES * TILE, 128), F32),
        ]
        + [pltpu.VMEM((TILES, TILE, QKV), BF16)] * 2
        + [pltpu.VMEM((NCHIP, MROWS, 2 * HW), BF16)] * 4
        + [pltpu.VMEM((NCHIP, MROWS, HW), BF16)] * 4
        + [
            pltpu.VMEM((2, NZ, TILES * TILE, HW), BF16),
            pltpu.VMEM((4, OCOLS, 256), F32),
        ]
        + [pltpu.VMEM((TILES, MROWS, 2 * HW), BF16)] * 2
        + [pltpu.VMEM((TILES, TILE, 2 * HW), F32)] * 2
        + [pltpu.VMEM((2 * TILES, 128), jnp.int32)]
        + [pltpu.SMEM((NSEQ, 2, 128), jnp.int32), pltpu.VMEM((NSEQ, 2, 128), jnp.int32)]
        + [pltpu.SMEM((2, NCHIP), jnp.int32)] * 5
        + [pltpu.SMEM((2, TILES), jnp.int32)]
        + [
            dma((TILES,)), dma((2, 36)), dma((2, 36)), dma((36,)), dma((36,)),
            dma((4,)), dma((4,)), dma,
            dma((2, NCHIP)), dma((2, NCHIP)), dma((2, NCHIP)), dma((2, NCHIP)),
            dma((2, 16)), dma((2, 16)), dma((NSEQ,)), dma((NSEQ,)),
        ],
        compiler_params=pltpu.CompilerParams(
            collective_id=0, has_side_effects=True, vmem_limit_bytes=60 * 1024 * 1024
        ),
    )(clusters, slots, tokens, qkv_weight, out_weight, centroids)


def solution(mesh):
    return jax.shard_map(
        on_device,
        mesh=mesh,
        in_specs=(
            P("seq", None),
            P("seq", "head"),
            P("head", "seq"),
            P("head", "seq", None),
            P("head", "seq"),
            P("head", "seq"),
        ),
        out_specs=(P("head", "seq"), P("head", "seq", None)),
        check_vma=False,
    )
```

```python
import functools

import jax
import jax.numpy as jnp
from jax import lax
from jax.experimental import pallas as pl
from jax.experimental.pallas import tpu as pltpu
from jax.sharding import PartitionSpec as P

MESH = pl.DeviceIdType.MESH
F32 = jnp.float32
BF16 = jnp.bfloat16

NX = 4
NZ = 8
NCHIP = 16
NSEQ = 32
TILE = 128
TILES = 8
HW = 128
QKV = 3 * HW
WROWS = 128
OROWS = 64
OCOLS = 512
MROWS = TILE + 8
LOG2E = 1.4426950408889634
LOGIT = 8.0 / 128


def kernel(
    clus_ref, slot_ref, tok_hbm, w_ref, wo_ref, cent_ref,
    out_ref, newc_ref,
    tok, wbuf, obuf, owt, rscale,
    qkv0, qkv1, stage0, stage1, recv0, recv1, ret0, ret1, back0, back1,
    gbuf, acc, msg0, msg1, own0, own1, late,
    codes_ref, cbuf, t_inv, t_lab, t_tile, t_par, t_lim, t_dst,
    tok_sem, w_send, w_recv, o_send, o_recv, sc_send, sc_recv, loc_sem,
    a_send, a_recv, r_send, r_recv, z_send, z_recv, m_send, m_recv,
):
    z = lax.axis_index("head")
    s = lax.axis_index("seq")
    c = s % 2
    q = s // 2
    x = q % NX
    y = q // NX
    u = y * (1 - c) + x * c
    v = x * (1 - c) + y * c
    qkv = (qkv0, qkv1)
    stage = (stage0, stage1)
    recv = (recv0, recv1)
    ret = (ret0, ret1)
    back = (back0, back1)
    msg = (msg0, msg1)
    own = (own0, own1)

    for t in range(TILES):
        pltpu.make_async_copy(
            tok_hbm.at[pl.ds(t * TILE, TILE)], tok.at[pl.ds(t * TILE, TILE)], tok_sem.at[t]
        ).start()
    own_w = pl.ds(pl.multiple_of(s * WROWS, WROWS), WROWS)
    wbuf[own_w, :] = w_ref[...]
    own_codes = clus_ref[...] * 2 + slot_ref[...]
    cbuf[s] = jnp.full((2, 128), -16, jnp.int32)
    cbuf[s, :, 0:TILES] = own_codes

    zg = s // 4
    barrier = pltpu.get_barrier_semaphore()

    def greet(i, carry):
        pl.semaphore_signal(barrier, inc=1, device_id=(z, (s + i) % NSEQ), device_id_type=MESH)
        return carry

    lax.fori_loop(1, NSEQ, greet, 0)
    pl.semaphore_signal(barrier, inc=1, device_id=((z + 1) % NZ, s), device_id_type=MESH)
    pl.semaphore_signal(barrier, inc=1, device_id=((z + NZ - 1) % NZ, s), device_id_type=MESH)

    @pl.when(zg != z)
    def _():
        for i in range(4):
            pl.semaphore_signal(barrier, inc=1, device_id=(zg, 4 * z + i), device_id_type=MESH)

    def scales(t):
        pltpu.make_async_copy(
            tok_hbm.at[pl.ds(t * TILE, TILE)], tok.at[pl.ds(t * TILE, TILE)], tok_sem.at[t]
        ).wait()

        def rows(i, carry):
            at = pl.ds(pl.multiple_of(t * TILE + i * 16, 16), 16)
            val = tok[at, :].astype(F32)
            mean = jnp.sum(val * val, axis=-1, keepdims=True) * (1.0 / tok.shape[1])
            rscale[at, :] = jnp.broadcast_to(lax.rsqrt(mean + 1e-5), (16, 128))
            return carry

        lax.fori_loop(0, TILE // 16, rows, 0)

    pl.semaphore_wait(barrier, jnp.where(zg != z, NSEQ - 1 + 2 + 4, NSEQ - 1 + 2))

    def slot(cc, uu, vv):
        uu = uu % NX
        vv = vv % NX
        yy = uu * (1 - cc) + vv * cc
        xx = vv * (1 - cc) + uu * cc
        return (yy * NX + xx) * 2 + cc

    class Gather:
        def __init__(self, buf, rows, send, recv_sem, cols=None):
            self.buf, self.rows, self.send, self.recv = buf, rows, send, recv_sem
            self.cols = slice(None) if cols is None else pl.ds(*cols)

        def copy(self, sl, part, dev, sem):
            rows = self.rows
            if part is None:
                ref = self.buf.at[pl.ds(pl.multiple_of(sl * rows, rows), rows), self.cols]
            else:
                half = rows // 2
                ref = self.buf.at[pl.ds(pl.multiple_of(sl * rows + part * half, half), half), self.cols]
            return pltpu.make_async_remote_copy(
                src_ref=ref, dst_ref=ref, send_sem=self.send.at[sem], recv_sem=self.recv.at[sem],
                device_id=(z, dev), device_id_type=MESH,
            )

        def v_copy(self, k, recv_side=False):
            if k == 0:
                sl = slot(c, u, v - 1 if recv_side else v)
                return self.copy(sl, None, slot(c, u, v + 1), 0)
            if k == 1:
                sl = slot(c, u, v + 1 if recv_side else v)
                return self.copy(sl, None, slot(c, u, v - 1), 1)
            if k == 2:
                sl = slot(c, u, v - 2 if recv_side else v - 1)
                return self.copy(sl, 0, slot(c, u, v + 1), 2)
            sl = slot(c, u, v + 2 if recv_side else v + 1)
            return self.copy(sl, 1, slot(c, u, v - 1), 3)

        def u_copy(self, j, k, recv_side=False):
            vv = v + (0, -1, 1, 2)[j]
            sem = 4 + 4 * j + k
            if k == 0:
                sl = slot(c, u - 1 if recv_side else u, vv)
                return self.copy(sl, None, slot(c, u + 1, v), sem)
            if k == 1:
                sl = slot(c, u + 1 if recv_side else u, vv)
                return self.copy(sl, None, slot(c, u - 1, v), sem)
            if k == 2:
                sl = slot(c, u - 2 if recv_side else u - 1, vv)
                return self.copy(sl, 0, slot(c, u + 1, v), sem)
            sl = slot(c, u + 2 if recv_side else u + 1, vv)
            return self.copy(sl, 1, slot(c, u - 1, v), sem)

        def c_copy(self, a, j, recv_side=False):
            du = (0, -1, 1, 2)[a]
            dv = (0, -1, 1, 2)[j]
            if recv_side:
                sl = slot(1 - c, v + du, u + dv)
            else:
                sl = slot(c, u + du, v + dv)
            return self.copy(sl, None, s + 1 - 2 * c, 20 + 4 * a + j)

        def steps(self):
            def first():
                self.v_copy(0).start()
                self.v_copy(1).start()
                self.u_copy(0, 0).start()
                self.u_copy(0, 1).start()
                self.c_copy(0, 0).start()

            def second():
                self.v_copy(0, True).wait_recv()
                self.v_copy(2).start()
                self.v_copy(1, True).wait_recv()
                self.v_copy(3).start()
                for j in (1, 2):
                    self.u_copy(j, 0).start()
                    self.u_copy(j, 1).start()
                    self.c_copy(0, j).start()

            def third():
                self.v_copy(2, True).wait_recv()
                self.v_copy(3, True).wait_recv()
                self.u_copy(3, 0).start()
                self.u_copy(3, 1).start()
                self.c_copy(0, 3).start()

            def along(j):
                def run():
                    self.u_copy(j, 0, True).wait_recv()
                    self.u_copy(j, 2).start()
                    self.c_copy(1, j).start()
                    self.u_copy(j, 1, True).wait_recv()
                    self.u_copy(j, 3).start()
                    self.c_copy(2, j).start()
                return run

            def far(j):
                def run():
                    self.u_copy(j, 2, True).wait_recv()
                    self.u_copy(j, 3, True).wait_recv()
                    self.c_copy(3, j).start()
                return run

            def last():
                for a in range(4):
                    for j in range(4):
                        self.c_copy(a, j, True).wait_recv()

            return [
                first, second, along(0), third, along(1), along(2), far(0), along(3),
                far(1), far(2), far(3), last,
            ]

        def drain(self):
            for k in range(4):
                self.v_copy(k).wait_send()
            for j in range(4):
                for k in range(4):
                    self.u_copy(j, k).wait_send()
            for a in range(4):
                for j in range(4):
                    self.c_copy(a, j).wait_send()

    gather_w = [
        Gather(wbuf, WROWS, w_send.at[h], w_recv.at[h], (h * QKV, QKV)) for h in range(2)
    ]
    gather_o = Gather(obuf, OROWS, o_send, o_recv)
    w_steps = [g.steps() for g in gather_w]
    o_steps = gather_o.steps()
    w_steps[0][0]()
    w_steps[1][0]()

    def code_copy(i, recv_side=False):
        at = (s + NSEQ - i) % NSEQ if recv_side else s
        return pltpu.make_async_remote_copy(
            src_ref=cbuf.at[at], dst_ref=cbuf.at[at], send_sem=m_send.at[i], recv_sem=m_recv.at[i],
            device_id=(z, (s + i) % NSEQ), device_id_type=MESH,
        )

    def send_codes(i, carry):
        code_copy(i).start()
        return carry

    lax.fori_loop(1, NSEQ, send_codes, 0)

    def codes_here():
        def one(i, carry):
            code_copy(i, True).wait_recv()
            return carry

        lax.fori_loop(1, NSEQ, one, 0)
        pltpu.make_async_copy(cbuf, codes_ref, loc_sem).start()

    def codes_read():
        pltpu.make_async_copy(cbuf, codes_ref, loc_sem).wait()

    def lateness():
        place = lax.broadcasted_iota(jnp.int32, (NSEQ, 128), 0) * TILES
        place = place + lax.broadcasted_iota(jnp.int32, (NSEQ, 128), 1)
        for h in range(2):
            codes = cbuf[:, h, :]
            for t in range(TILES):
                mine = own_codes[h:h + 1, t:t + 1]
                want = jnp.broadcast_to(mine + 1 - 2 * (mine % 2), (NSEQ, 128))
                hit = (codes == want) & (place < s * TILES + t)
                some = jnp.max(jnp.where(hit, 1, 0), axis=0, keepdims=True)
                some = jnp.max(some, axis=1, keepdims=True)
                late[h * TILES + t:h * TILES + t + 1, :] = jnp.broadcast_to(some, (1, 128))

    own_o = pl.multiple_of(s * OROWS, OROWS)

    def scatter(i):
        return pltpu.make_async_remote_copy(
            src_ref=wo_ref.at[pl.ds(i * OROWS, OROWS)],
            dst_ref=obuf.at[pl.ds(pl.multiple_of((4 * z + i) * OROWS, OROWS), OROWS),
                            pl.ds(pl.multiple_of((s % 4) * 128, 128), 128)],
            send_sem=sc_send.at[i], recv_sem=sc_recv.at[s % 4],
            device_id=(zg, 4 * z + i), device_id_type=MESH,
        )

    def scattered(j):
        return pltpu.make_async_remote_copy(
            src_ref=wo_ref.at[pl.ds(j * OROWS, OROWS)],
            dst_ref=obuf.at[pl.ds(own_o, OROWS), pl.ds(j * 128, 128)],
            send_sem=sc_send.at[j], recv_sem=sc_recv.at[j],
            device_id=(zg, 4 * z + j), device_id_type=MESH,
        )

    for i in range(4):
        is_self = (zg == z) & (s % 4 == i)

        @pl.when(jnp.logical_not(is_self))
        def _(i=i):
            scatter(i).start()

        @pl.when(is_self)
        def _(i=i):
            cp = pltpu.make_async_copy(
                wo_ref.at[pl.ds(i * OROWS, OROWS)],
                obuf.at[pl.ds(own_o, OROWS), pl.ds(i * 128, 128)],
                loc_sem,
            )
            cp.start()
            cp.wait()

    def tables(h):
        def per_offset(d, carry):
            dy, dx = d // NX, d % NX
            src = (((y + NX - dy) % NX) * NX + (x + NX - dx) % NX) * 2 + (c + h) % 2
            dst = (((y + dy) % NX) * NX + (x + dx) % NX) * 2 + (c + h) % 2
            lab = jnp.int32(-1)
            til = jnp.int32(0)
            inv = jnp.int32(0)
            for t in range(TILES):
                code = codes_ref[src, h, t]
                hit = (code // 16) == s
                lab = jnp.where(hit, code % 16, lab)
                til = jnp.where(hit, t, til)
                mine = codes_ref[s, h, t]
                inv = jnp.where((mine // 16) == dst, t, inv)
            t_lab[h, d] = lab
            t_tile[h, d] = src * TILES + til
            t_inv[h, d] = inv
            return carry

        lax.fori_loop(0, NCHIP, per_offset, 0)

        def per_arrival(d, carry):
            lab = t_lab[h, d]
            want = jnp.where(lab < 0, -2, lab + 1 - 2 * (lab % 2))
            til = t_tile[h, d]
            par = d
            lim = jnp.int32(TILE)
            for e in range(NCHIP):
                hit = t_lab[h, e] == want
                par = jnp.where(hit, e, par)
                lim = jnp.where(hit & (t_tile[h, e] < til), 2 * TILE, lim)
            t_par[h, d] = par
            t_lim[h, d] = lim
            return carry

        lax.fori_loop(0, NCHIP, per_arrival, 0)
        for t in range(TILES):
            owner = codes_ref[s, h, t] // 32
            oy, ox = owner // NX, owner % NX
            t_dst[h, t] = ((oy + NX - y) % NX) * NX + (ox + NX - x) % NX

    lag = 4
    for k in range(1, 12):
        w_steps[0][k]()
        if k <= TILES:
            scales(k - 1)
        if k - lag >= 1:
            w_steps[1][k - lag]()
        if k == 5:
            codes_here()
            lateness()
        if k == 8:
            codes_read()
        if k in (8, 9):
            tables(k - 8)

    def project(h, m):
        if True:
            at = pl.ds(pl.multiple_of(m * 256, 256), 256)
            val = jnp.dot(tok[at, :], wbuf[:, h * QKV:(h + 1) * QKV], preferred_element_type=F32)
            rs = rscale[at, :]
            unit = []
            for p in range(2):
                vf = (val[:, p * HW:(p + 1) * HW] * rs).astype(BF16).astype(F32)
                mean = jnp.mean(vf * vf, axis=-1, keepdims=True)
                unit.append(vf * lax.rsqrt(mean + 1e-6))
            query = (unit[0] * (LOGIT * LOG2E)).astype(BF16)
            key = unit[1].astype(BF16)
            value = (val[:, 2 * HW:] * rs).astype(BF16)
            row8 = lax.broadcasted_iota(jnp.int32, (8, HW), 0)
            for i in range(2):
                t = m * 2 + i
                part = slice(i * TILE, (i + 1) * TILE)
                qkv[h][t, :, :HW] = query[part]
                qkv[h][t, :, HW:2 * HW] = key[part]
                qkv[h][t, :, 2 * HW:] = value[part]
                is_late = jnp.broadcast_to(late[h * TILES + t:h * TILES + t + 1, :], (TILE, HW)) > 0
                msg[h][t, :TILE, :HW] = jnp.where(is_late, query[part], key[part])
                msg[h][t, :TILE, HW:] = value[part]
                tot = jnp.sum(unit[1][part], axis=0, keepdims=True)
                high = tot.astype(BF16).astype(F32)
                extra = jnp.where(row8 == 0, high, jnp.where(row8 == 1, tot - high, 0.0))
                msg[h][t, TILE:, :HW] = extra.astype(BF16)
                msg[h][t, TILE:, HW:] = jnp.zeros((8, HW), BF16)

    def a_copy(h, d, recv_side=False):
        dy, dx = d // NX, d % NX
        dev = (((y + dy) % NX) * NX + (x + dx) % NX) * 2 + (c + h) % 2
        return pltpu.make_async_remote_copy(
            src_ref=stage[h].at[d], dst_ref=recv[h].at[d],
            send_sem=a_send.at[h, d], recv_sem=a_recv.at[h, d],
            device_id=(z, dev), device_id_type=MESH,
        )

    def r_copy(h, d):
        dy, dx = d // NX, d % NX
        dev = (((y + NX - dy) % NX) * NX + (x + NX - dx) % NX) * 2 + (c + h) % 2
        return pltpu.make_async_remote_copy(
            src_ref=ret[h].at[d], dst_ref=back[h].at[d],
            send_sem=r_send.at[h, d], recv_sem=r_recv.at[h, d],
            device_id=(z, dev), device_id_type=MESH,
        )

    def stage_tiles(h):
        if h == 0:
            recv[0][0] = msg[0][t_inv[0, 0]]

        def one(d, carry):
            stage[h][d] = msg[h][t_inv[h, d]]
            return carry

        lax.fori_loop(1 - h, NCHIP, one, 0)

    def send_tiles(h):
        def one(d, carry):
            a_copy(h, d).start()
            return carry

        lax.fori_loop(1 - h, NCHIP, one, 0)

    def arrivals(h):
        def one(d, carry):
            a_copy(h, d).wait_recv()
            return carry

        lax.fori_loop(1 - h, NCHIP, one, 0)

    row = lax.broadcasted_iota(jnp.int32, (TILE, TILE), 0)
    col = lax.broadcasted_iota(jnp.int32, (TILE, TILE), 1)
    ones = jnp.ones((TILE, HW), BF16)
    contract_last = (((1,), (1,)), ((), ()))

    def attend_own(h):
        def one(t, carry):
            mine = qkv[h][t]
            logits = lax.dot_general(
                mine[:, :HW], mine[:, HW:2 * HW], contract_last, preferred_element_type=F32
            )
            probs = jnp.where(col <= row, jnp.exp2(logits), 0.0).astype(BF16)
            own[h][t] = jnp.dot(
                probs, jnp.concatenate([mine[:, 2 * HW:], ones], axis=1),
                preferred_element_type=F32,
            )
            return carry

        lax.fori_loop(0, TILES, one, 0, unroll=4)

    def attend(h):
        row8 = lax.broadcasted_iota(jnp.int32, (8, TILE), 0)
        ones8 = jnp.ones((8, TILE), BF16)

        def one(d, store):
            earlier = recv[h][t_par[h, d]]
            logits = lax.dot_general(
                recv[h][d, :TILE, :HW], earlier[:TILE, :HW], contract_last,
                preferred_element_type=F32,
            )
            logits = jnp.where(col < t_lim[h, d] - TILE, logits, 0.0)
            probs = jnp.exp2(logits).astype(BF16)
            both = jnp.dot(
                probs, jnp.concatenate([earlier[:TILE, HW:], ones], axis=1),
                preferred_element_type=F32,
            )
            tot = lax.dot_general(ones8, probs, contract_last, preferred_element_type=F32)
            high = tot.astype(BF16).astype(F32)
            extra = jnp.where(row8 == 0, high, jnp.where(row8 == 1, tot - high, 0.0))
            store[h][d, :TILE] = (both[:, :HW] / both[:, HW:]).astype(BF16)
            store[h][d, TILE:] = extra.astype(BF16)

        if h == 0:
            one(0, back)

        group = 5 if h == 0 else 4

        def loop(g, carry):
            for i in range(group):
                one(1 - h + g * group + i, ret)
            for i in range(group):
                r_copy(h, 1 - h + g * group + i).start()
            return carry

        lax.fori_loop(0, (NCHIP - 1 + h) // group, loop, 0)

    def centroids(h):
        rows8 = lax.broadcasted_iota(jnp.int32, (8, HW), 0)

        def one(d, carry):
            sums, counts = carry
            cl = (t_lab[h, d] + 2) // 2 - 1
            hit = rows8 == cl
            tot = jnp.sum(recv[h][d, TILE:, :HW].astype(F32), axis=0, keepdims=True)
            sums = sums + jnp.where(hit, jnp.broadcast_to(tot, (8, HW)), 0.0)
            counts = counts + jnp.where(hit, float(TILE), 0.0)
            return sums, counts

        zero = jnp.zeros((8, HW), F32)
        sums, counts = lax.fori_loop(0, NCHIP, one, (zero, zero))
        cent = cent_ref[h]
        means = sums / jnp.maximum(counts, 1.0)
        newc_ref[h] = cent + 0.25 * jnp.where(counts > 0, means - cent, 0.0)

    def come_home(h):
        def one(d, carry):
            r_copy(h, d).wait_recv()
            return carry

        lax.fori_loop(1 - h, NCHIP, one, 0)
        for t in range(TILES):
            far = back[h][t_dst[h, t]]
            is_late = jnp.broadcast_to(late[h * TILES + t:h * TILES + t + 1, :], (TILE, HW)) > 0
            weight = lax.dot_general(
                far[TILE:], jnp.ones((8, HW), BF16), (((0,), (0,)), ((), ())),
                preferred_element_type=F32,
            )
            top = own[h][t, :, :HW] + jnp.where(is_late, weight * far[:TILE].astype(F32), 0.0)
            low = own[h][t, :, HW:] + jnp.where(is_late, weight, 0.0)
            gbuf[h, z, pl.ds(t * TILE, TILE)] = (top / low).astype(BF16)

    half = TILES * TILE // 2

    def z_copy(h, way, k, j, recv_side=False):
        sign = 1 if way == 0 else -1
        at = z - sign * (k - 1)
        if recv_side:
            at = at - sign
        ref = gbuf.at[h, (at + 2 * NZ) % NZ, pl.ds(j * half, half)]
        idx = way * 8 + (k - 1) * 2 + j
        return pltpu.make_async_remote_copy(
            src_ref=ref, dst_ref=ref, send_sem=z_send.at[h, idx], recv_sem=z_recv.at[h, idx],
            device_id=((z + sign + NZ) % NZ, s), device_id_type=MESH,
        )

    def z_parts(k):
        if k < 4:
            return [(way, j) for j in range(2) for way in range(2)]
        return [(0, 0), (1, 1)]

    def z_first(h):
        for way, j in z_parts(1):
            z_copy(h, way, 1, j).start()

    def z_step(h, k):
        nxt = z_parts(k + 1) if k < 4 else []
        for way, j in z_parts(k):
            z_copy(h, way, k, j, True).wait_recv()
            if (way, j) in nxt:
                z_copy(h, way, k + 1, j).start()

    def z_drain(h):
        for k in range(1, 5):
            for way, j in z_parts(k):
                z_copy(h, way, k, j).wait_send()

    def multiply(h, ga, gb, mode):
        ga = (z + ga) % NZ
        gb = (z + gb) % NZ

        rhs = jnp.concatenate([gbuf[h, ga], gbuf[h, gb]], axis=1)
        for m in range(2):
            part = slice(m * 256, (m + 1) * 256)
            lhs = jnp.concatenate([owt[h, ga, part], owt[h, gb, part]], axis=1)
            val = lax.dot_general(lhs, rhs, (((1,), (1,)), ((), ())), preferred_element_type=F32)
            if mode != "first":
                val = val + acc[m]
            if mode == "last":
                out_ref[part, :] = val.astype(BF16)
            else:
                acc[m] = val

    rest = w_steps[1][12 - lag:]
    for m in range(4):
        project(0, m)
        if m < 3 and rest:
            rest.pop(0)()
    stage_tiles(0)
    send_tiles(0)
    for f in rest:
        f()
    for m in range(4):
        project(1, m)
    stage_tiles(1)
    attend_own(0)
    attend_own(1)
    for j in range(4):
        not_self = (zg != z) | (s % 4 != j)

        @pl.when(not_self)
        def _(j=j):
            scattered(j).wait_recv()

    arrivals(0)
    attend(0)
    send_tiles(1)
    come_home(0)
    z_first(0)
    o_steps[0]()
    z_step(0, 1)
    o_steps[1]()
    o_steps[2]()
    z_step(0, 2)
    o_steps[3]()
    o_steps[4]()
    arrivals(1)
    attend(1)
    z_step(0, 3)
    o_steps[5]()
    o_steps[6]()
    o_steps[7]()
    come_home(1)
    z_first(1)
    for f in o_steps[8:]:
        f()
    centroids(0)
    centroids(1)
    for g in range(NZ):
        for h in range(2):
            at = (g * 2 + h) * HW
            owt[h, g] = obuf[at:at + HW, :].astype(F32).T.astype(BF16)
    z_step(0, 4)
    multiply(0, 0, 1, "first")
    z_step(1, 1)
    multiply(0, 7, 2, "mid")
    multiply(0, 6, 3, "mid")
    multiply(0, 5, 4, "mid")
    multiply(1, 1, 7, "mid")
    z_step(1, 2)
    multiply(1, 2, 6, "mid")
    z_step(1, 3)
    multiply(1, 3, 5, "mid")
    z_step(1, 4)
    multiply(1, 0, 4, "last")

    gather_w[0].drain()
    gather_w[1].drain()
    gather_o.drain()

    def codes_sent(i, carry):
        code_copy(i).wait_send()
        return carry

    lax.fori_loop(1, NSEQ, codes_sent, 0)
    for i in range(4):
        @pl.when((zg != z) | (s % 4 != i))
        def _(i=i):
            scatter(i).wait_send()

    for h in range(2):
        def sent(d, carry, h=h):
            a_copy(h, d).wait_send()
            r_copy(h, d).wait_send()
            return carry

        lax.fori_loop(1 - h, NCHIP, sent, 0)
        z_drain(h)


def on_device(tokens, qkv_weight, out_weight, centroids, clusters, slots):
    vmem = pl.BlockSpec(memory_space=pltpu.VMEM)
    dma = pltpu.SemaphoreType.DMA
    return pl.pallas_call(
        kernel,
        out_shape=(
            jax.ShapeDtypeStruct((OCOLS, TILES * TILE), BF16),
            jax.ShapeDtypeStruct(centroids.shape, F32),
        ),
        in_specs=[
            vmem, vmem,
            pl.BlockSpec(memory_space=pl.ANY),
            vmem, vmem, vmem,
        ],
        out_specs=(vmem, vmem),
        scratch_shapes=[
            pltpu.VMEM(tokens.shape, BF16),
            pltpu.VMEM((NSEQ * WROWS, 2 * QKV), BF16),
            pltpu.VMEM((NSEQ * OROWS, OCOLS), BF16),
            pltpu.VMEM((2, NZ, OCOLS, HW), BF16),
            pltpu.VMEM((TILES * TILE, 128), F32),
        ]
        + [pltpu.VMEM((TILES, TILE, QKV), BF16)] * 2
        + [pltpu.VMEM((NCHIP, MROWS, 2 * HW), BF16)] * 4
        + [pltpu.VMEM((NCHIP, MROWS, HW), BF16)] * 4
        + [
            pltpu.VMEM((2, NZ, TILES * TILE, HW), BF16),
            pltpu.VMEM((2, 256, TILES * TILE), F32),
        ]
        + [pltpu.VMEM((TILES, MROWS, 2 * HW), BF16)] * 2
        + [pltpu.VMEM((TILES, TILE, 2 * HW), F32)] * 2
        + [pltpu.VMEM((2 * TILES, 128), jnp.int32)]
        + [pltpu.SMEM((NSEQ, 2, 128), jnp.int32), pltpu.VMEM((NSEQ, 2, 128), jnp.int32)]
        + [pltpu.SMEM((2, NCHIP), jnp.int32)] * 5
        + [pltpu.SMEM((2, TILES), jnp.int32)]
        + [
            dma((TILES,)), dma((2, 36)), dma((2, 36)), dma((36,)), dma((36,)),
            dma((4,)), dma((4,)), dma,
            dma((2, NCHIP)), dma((2, NCHIP)), dma((2, NCHIP)), dma((2, NCHIP)),
            dma((2, 16)), dma((2, 16)), dma((NSEQ,)), dma((NSEQ,)),
        ],
        compiler_params=pltpu.CompilerParams(
            collective_id=0, has_side_effects=True, vmem_limit_bytes=60 * 1024 * 1024
        ),
    )(clusters, slots, tokens, qkv_weight, out_weight, centroids)


def solution(mesh):
    return jax.shard_map(
        on_device,
        mesh=mesh,
        in_specs=(
            P("seq", None),
            P("seq", "head"),
            P("head", "seq"),
            P("head", "seq", None),
            P("head", "seq"),
            P("head", "seq"),
        ),
        out_specs=(P("head", "seq"), P("head", "seq", None)),
        check_vma=False,
    )
```

```python
import functools

import jax
import jax.numpy as jnp
from jax import lax
from jax.experimental import pallas as pl
from jax.experimental.pallas import tpu as pltpu
from jax.sharding import PartitionSpec as P

MESH = pl.DeviceIdType.MESH
F32 = jnp.float32
BF16 = jnp.bfloat16

NX = 4
NZ = 8
NCHIP = 16
NSEQ = 32
TILE = 128
TILES = 8
HW = 128
QKV = 3 * HW
WROWS = 128
OROWS = 64
OCOLS = 512
MROWS = TILE + 8
LOG2E = 1.4426950408889634
LOGIT = 8.0 / 128


def kernel(
    clus_ref, slot_ref, tok_hbm, w_ref, wo_ref, cent_ref,
    out_ref, newc_ref,
    tok, wbuf, obuf, owt, rscale,
    qkv0, qkv1, stage0, stage1, recv0, recv1, ret0, ret1, back0, back1,
    gbuf, acc, msg0, msg1, own0, own1, late,
    codes_ref, cbuf, t_inv, t_lab, t_tile, t_par, t_lim, t_dst,
    tok_sem, w_send, w_recv, o_send, o_recv, sc_send, sc_recv, loc_sem,
    a_send, a_recv, r_send, r_recv, z_send, z_recv, m_send, m_recv,
):
    z = lax.axis_index("head")
    s = lax.axis_index("seq")
    c = s % 2
    q = s // 2
    x = q % NX
    y = q // NX
    u = y * (1 - c) + x * c
    v = x * (1 - c) + y * c
    qkv = (qkv0, qkv1)
    stage = (stage0, stage1)
    recv = (recv0, recv1)
    ret = (ret0, ret1)
    back = (back0, back1)
    msg = (msg0, msg1)
    own = (own0, own1)

    for t in range(TILES):
        pltpu.make_async_copy(
            tok_hbm.at[pl.ds(t * TILE, TILE)], tok.at[pl.ds(t * TILE, TILE)], tok_sem.at[t]
        ).start()
    own_w = pl.ds(pl.multiple_of(s * WROWS, WROWS), WROWS)
    wbuf[own_w, :] = w_ref[...]
    own_codes = clus_ref[...] * 2 + slot_ref[...]
    cbuf[s] = jnp.full((2, 128), -16, jnp.int32)
    cbuf[s, :, 0:TILES] = own_codes

    zg = s // 4
    barrier = pltpu.get_barrier_semaphore()

    def greet(i, carry):
        pl.semaphore_signal(barrier, inc=1, device_id=(z, (s + i) % NSEQ), device_id_type=MESH)
        return carry

    lax.fori_loop(1, NSEQ, greet, 0)
    pl.semaphore_signal(barrier, inc=1, device_id=((z + 1) % NZ, s), device_id_type=MESH)
    pl.semaphore_signal(barrier, inc=1, device_id=((z + NZ - 1) % NZ, s), device_id_type=MESH)

    @pl.when(zg != z)
    def _():
        for i in range(4):
            pl.semaphore_signal(barrier, inc=1, device_id=(zg, 4 * z + i), device_id_type=MESH)

    def scales(t):
        pltpu.make_async_copy(
            tok_hbm.at[pl.ds(t * TILE, TILE)], tok.at[pl.ds(t * TILE, TILE)], tok_sem.at[t]
        ).wait()

        def rows(i, carry):
            at = pl.ds(pl.multiple_of(t * TILE + i * 16, 16), 16)
            val = tok[at, :].astype(F32)
            mean = jnp.sum(val * val, axis=-1, keepdims=True) * (1.0 / tok.shape[1])
            rscale[at, :] = jnp.broadcast_to(lax.rsqrt(mean + 1e-5), (16, 128))
            return carry

        lax.fori_loop(0, TILE // 16, rows, 0, unroll=4)

    pl.semaphore_wait(barrier, jnp.where(zg != z, NSEQ - 1 + 2 + 4, NSEQ - 1 + 2))

    def slot(cc, uu, vv):
        uu = uu % NX
        vv = vv % NX
        yy = uu * (1 - cc) + vv * cc
        xx = vv * (1 - cc) + uu * cc
        return (yy * NX + xx) * 2 + cc

    class Gather:
        def __init__(self, buf, rows, send, recv_sem, cols=None):
            self.buf, self.rows, self.send, self.recv = buf, rows, send, recv_sem
            self.cols = slice(None) if cols is None else pl.ds(*cols)

        def copy(self, sl, part, dev, sem):
            rows = self.rows
            if part is None:
                ref = self.buf.at[pl.ds(pl.multiple_of(sl * rows, rows), rows), self.cols]
            else:
                half = rows // 2
                ref = self.buf.at[pl.ds(pl.multiple_of(sl * rows + part * half, half), half), self.cols]
            return pltpu.make_async_remote_copy(
                src_ref=ref, dst_ref=ref, send_sem=self.send.at[sem], recv_sem=self.recv.at[sem],
                device_id=(z, dev), device_id_type=MESH,
            )

        def v_copy(self, k, recv_side=False):
            if k == 0:
                sl = slot(c, u, v - 1 if recv_side else v)
                return self.copy(sl, None, slot(c, u, v + 1), 0)
            if k == 1:
                sl = slot(c, u, v + 1 if recv_side else v)
                return self.copy(sl, None, slot(c, u, v - 1), 1)
            sl = slot(c, u, v + 2 if recv_side else v)
            return self.copy(sl, None, slot(c, u, v + 2), 2)

        def u_copy(self, j, k, recv_side=False):
            vv = v + (0, -1, 1, 2)[j]
            sem = 4 + 4 * j + k
            if k == 0:
                sl = slot(c, u - 1 if recv_side else u, vv)
                return self.copy(sl, None, slot(c, u + 1, v), sem)
            if k == 1:
                sl = slot(c, u + 1 if recv_side else u, vv)
                return self.copy(sl, None, slot(c, u - 1, v), sem)
            if k == 2:
                sl = slot(c, u - 2 if recv_side else u - 1, vv)
                return self.copy(sl, 0, slot(c, u + 1, v), sem)
            sl = slot(c, u + 2 if recv_side else u + 1, vv)
            return self.copy(sl, 1, slot(c, u - 1, v), sem)

        def c_copy(self, a, j, recv_side=False):
            du = (0, -1, 1, 2)[a]
            dv = (0, -1, 1, 2)[j]
            if recv_side:
                sl = slot(1 - c, v + du, u + dv)
            else:
                sl = slot(c, u + du, v + dv)
            return self.copy(sl, None, s + 1 - 2 * c, 20 + 4 * a + j)

        def steps(self):
            def first():
                self.v_copy(0).start()
                self.v_copy(1).start()
                self.v_copy(2).start()
                self.u_copy(0, 0).start()
                self.u_copy(0, 1).start()
                self.c_copy(0, 0).start()

            def second():
                self.v_copy(0, True).wait_recv()
                self.v_copy(1, True).wait_recv()
                for j in (1, 2):
                    self.u_copy(j, 0).start()
                    self.u_copy(j, 1).start()
                    self.c_copy(0, j).start()

            def third():
                self.v_copy(2, True).wait_recv()
                self.u_copy(3, 0).start()
                self.u_copy(3, 1).start()
                self.c_copy(0, 3).start()

            def along(j):
                def run():
                    self.u_copy(j, 0, True).wait_recv()
                    self.u_copy(j, 2).start()
                    self.c_copy(1, j).start()
                    self.u_copy(j, 1, True).wait_recv()
                    self.u_copy(j, 3).start()
                    self.c_copy(2, j).start()
                return run

            def far(j):
                def run():
                    self.u_copy(j, 2, True).wait_recv()
                    self.u_copy(j, 3, True).wait_recv()
                    self.c_copy(3, j).start()
                return run

            def last():
                for a in range(4):
                    for j in range(4):
                        self.c_copy(a, j, True).wait_recv()

            return [
                first, second, along(0), third, along(1), along(2), far(0), along(3),
                far(1), far(2), far(3), last,
            ]

        def drain(self):
            for k in range(3):
                self.v_copy(k).wait_send()
            for j in range(4):
                for k in range(4):
                    self.u_copy(j, k).wait_send()
            for a in range(4):
                for j in range(4):
                    self.c_copy(a, j).wait_send()

    gather_w = [
        Gather(wbuf, WROWS, w_send.at[h], w_recv.at[h], (h * QKV, QKV)) for h in range(2)
    ]
    gather_o = Gather(obuf, OROWS, o_send, o_recv)
    w_steps = [g.steps() for g in gather_w]
    o_steps = gather_o.steps()
    w_steps[0][0]()
    w_steps[1][0]()

    def code_copy(i, recv_side=False):
        at = (s + NSEQ - i) % NSEQ if recv_side else s
        return pltpu.make_async_remote_copy(
            src_ref=cbuf.at[at], dst_ref=cbuf.at[at], send_sem=m_send.at[i], recv_sem=m_recv.at[i],
            device_id=(z, (s + i) % NSEQ), device_id_type=MESH,
        )

    def send_codes(i, carry):
        code_copy(i).start()
        return carry

    lax.fori_loop(1, NSEQ, send_codes, 0)

    def codes_here():
        def one(i, carry):
            code_copy(i, True).wait_recv()
            return carry

        lax.fori_loop(1, NSEQ, one, 0)
        pltpu.make_async_copy(cbuf, codes_ref, loc_sem).start()

    def codes_read():
        pltpu.make_async_copy(cbuf, codes_ref, loc_sem).wait()

    def lateness(h):
        place = lax.broadcasted_iota(jnp.int32, (NSEQ, 128), 0) * TILES
        place = place + lax.broadcasted_iota(jnp.int32, (NSEQ, 128), 1)
        if True:
            codes = cbuf[:, h, :]
            for t in range(TILES):
                mine = own_codes[h:h + 1, t:t + 1]
                want = jnp.broadcast_to(mine + 1 - 2 * (mine % 2), (NSEQ, 128))
                hit = (codes == want) & (place < s * TILES + t)
                some = jnp.max(jnp.where(hit, 1, 0), axis=0, keepdims=True)
                some = jnp.max(some, axis=1, keepdims=True)
                late[h * TILES + t:h * TILES + t + 1, :] = jnp.broadcast_to(some, (1, 128))

    own_o = pl.multiple_of(s * OROWS, OROWS)

    def scatter(i):
        return pltpu.make_async_remote_copy(
            src_ref=wo_ref.at[pl.ds(i * OROWS, OROWS)],
            dst_ref=obuf.at[pl.ds(pl.multiple_of((4 * z + i) * OROWS, OROWS), OROWS),
                            pl.ds(pl.multiple_of((s % 4) * 128, 128), 128)],
            send_sem=sc_send.at[i], recv_sem=sc_recv.at[s % 4],
            device_id=(zg, 4 * z + i), device_id_type=MESH,
        )

    def scattered(j):
        return pltpu.make_async_remote_copy(
            src_ref=wo_ref.at[pl.ds(j * OROWS, OROWS)],
            dst_ref=obuf.at[pl.ds(own_o, OROWS), pl.ds(j * 128, 128)],
            send_sem=sc_send.at[j], recv_sem=sc_recv.at[j],
            device_id=(zg, 4 * z + j), device_id_type=MESH,
        )

    for i in range(4):
        is_self = (zg == z) & (s % 4 == i)

        @pl.when(jnp.logical_not(is_self))
        def _(i=i):
            scatter(i).start()

        @pl.when(is_self)
        def _(i=i):
            cp = pltpu.make_async_copy(
                wo_ref.at[pl.ds(i * OROWS, OROWS)],
                obuf.at[pl.ds(own_o, OROWS), pl.ds(i * 128, 128)],
                loc_sem,
            )
            cp.start()
            cp.wait()

    def send_table(h):
        def per_offset(d, carry):
            dy, dx = d // NX, d % NX
            dst = (((y + dy) % NX) * NX + (x + dx) % NX) * 2 + (c + h) % 2
            inv = jnp.int32(0)
            for t in range(TILES):
                mine = codes_ref[s, h, t]
                inv = jnp.where((mine // 16) == dst, t, inv)
            t_inv[h, d] = inv
            return carry

        lax.fori_loop(0, NCHIP, per_offset, 0)

    def tables(h):
        def per_offset(d, carry):
            dy, dx = d // NX, d % NX
            src = (((y + NX - dy) % NX) * NX + (x + NX - dx) % NX) * 2 + (c + h) % 2
            lab = jnp.int32(-1)
            til = jnp.int32(0)
            for t in range(TILES):
                code = codes_ref[src, h, t]
                hit = (code // 16) == s
                lab = jnp.where(hit, code % 16, lab)
                til = jnp.where(hit, t, til)
            t_lab[h, d] = lab
            t_tile[h, d] = src * TILES + til
            return carry

        lax.fori_loop(0, NCHIP, per_offset, 0)

        def per_arrival(d, carry):
            lab = t_lab[h, d]
            want = jnp.where(lab < 0, -2, lab + 1 - 2 * (lab % 2))
            til = t_tile[h, d]
            par = d
            lim = jnp.int32(TILE)
            for e in range(NCHIP):
                hit = t_lab[h, e] == want
                par = jnp.where(hit, e, par)
                lim = jnp.where(hit & (t_tile[h, e] < til), 2 * TILE, lim)
            t_par[h, d] = par
            t_lim[h, d] = lim
            return carry

        lax.fori_loop(0, NCHIP, per_arrival, 0)
        for t in range(TILES):
            owner = codes_ref[s, h, t] // 32
            oy, ox = owner // NX, owner % NX
            t_dst[h, t] = ((oy + NX - y) % NX) * NX + (ox + NX - x) % NX

    lag = 4
    for k in range(1, 12):
        w_steps[0][k]()
        if k <= TILES:
            scales(k - 1)
        if k - lag >= 1:
            w_steps[1][k - lag]()
        if k == 5:
            codes_here()
            lateness(0)
        if k == 8:
            codes_read()
        if k == 8:
            send_table(0)

    def project(h, m):
        if True:
            at = pl.ds(pl.multiple_of(m * 256, 256), 256)
            val = jnp.dot(tok[at, :], wbuf[:, h * QKV:(h + 1) * QKV], preferred_element_type=F32)
            rs = rscale[at, :]
            unit = []
            for p in range(2):
                vf = (val[:, p * HW:(p + 1) * HW] * rs).astype(BF16).astype(F32)
                mean = jnp.mean(vf * vf, axis=-1, keepdims=True)
                unit.append(vf * lax.rsqrt(mean + 1e-6))
            query = (unit[0] * (LOGIT * LOG2E)).astype(BF16)
            key = unit[1].astype(BF16)
            value = (val[:, 2 * HW:] * rs).astype(BF16)
            row8 = lax.broadcasted_iota(jnp.int32, (8, HW), 0)
            for i in range(2):
                t = m * 2 + i
                part = slice(i * TILE, (i + 1) * TILE)
                qkv[h][t, :, :HW] = query[part]
                qkv[h][t, :, HW:2 * HW] = key[part]
                qkv[h][t, :, 2 * HW:] = value[part]
                is_late = jnp.broadcast_to(late[h * TILES + t:h * TILES + t + 1, :], (TILE, HW)) > 0
                msg[h][t, :TILE, :HW] = jnp.where(is_late, query[part], key[part])
                msg[h][t, :TILE, HW:] = value[part]
                tot = jnp.sum(unit[1][part], axis=0, keepdims=True)
                high = tot.astype(BF16).astype(F32)
                extra = jnp.where(row8 == 0, high, jnp.where(row8 == 1, tot - high, 0.0))
                msg[h][t, TILE:, :HW] = extra.astype(BF16)
                msg[h][t, TILE:, HW:] = jnp.zeros((8, HW), BF16)

    def a_copy(h, d, recv_side=False):
        dy, dx = d // NX, d % NX
        dev = (((y + dy) % NX) * NX + (x + dx) % NX) * 2 + (c + h) % 2
        return pltpu.make_async_remote_copy(
            src_ref=stage[h].at[d], dst_ref=recv[h].at[d],
            send_sem=a_send.at[h, d], recv_sem=a_recv.at[h, d],
            device_id=(z, dev), device_id_type=MESH,
        )

    def r_copy(h, d):
        dy, dx = d // NX, d % NX
        dev = (((y + NX - dy) % NX) * NX + (x + NX - dx) % NX) * 2 + (c + h) % 2
        return pltpu.make_async_remote_copy(
            src_ref=ret[h].at[d], dst_ref=back[h].at[d],
            send_sem=r_send.at[h, d], recv_sem=r_recv.at[h, d],
            device_id=(z, dev), device_id_type=MESH,
        )

    def stage_tiles(h):
        if h == 0:
            recv[0][0] = msg[0][t_inv[0, 0]]

        def one(d, carry):
            stage[h][d] = msg[h][t_inv[h, d]]
            return carry

        lax.fori_loop(1 - h, NCHIP, one, 0)

    def send_tiles(h):
        def one(d, carry):
            a_copy(h, d).start()
            return carry

        lax.fori_loop(1 - h, NCHIP, one, 0)

    def arrivals(h):
        def one(d, carry):
            a_copy(h, d).wait_recv()
            return carry

        lax.fori_loop(1 - h, NCHIP, one, 0)

    row = lax.broadcasted_iota(jnp.int32, (TILE, TILE), 0)
    col = lax.broadcasted_iota(jnp.int32, (TILE, TILE), 1)
    ones = jnp.ones((TILE, HW), BF16)
    contract_last = (((1,), (1,)), ((), ()))

    def attend_own(h):
        def one(t, carry):
            mine = qkv[h][t]
            logits = lax.dot_general(
                mine[:, :HW], mine[:, HW:2 * HW], contract_last, preferred_element_type=F32
            )
            probs = jnp.where(col <= row, jnp.exp2(logits), 0.0).astype(BF16)
            own[h][t] = jnp.dot(
                probs, jnp.concatenate([mine[:, 2 * HW:], ones], axis=1),
                preferred_element_type=F32,
            )
            return carry

        lax.fori_loop(0, TILES, one, 0, unroll=4)

    def attend(h):
        row8 = lax.broadcasted_iota(jnp.int32, (8, TILE), 0)
        ones8 = jnp.ones((8, TILE), BF16)

        def one(d, store):
            earlier = recv[h][t_par[h, d]]
            logits = lax.dot_general(
                recv[h][d, :TILE, :HW], earlier[:TILE, :HW], contract_last,
                preferred_element_type=F32,
            )
            logits = jnp.where(col < t_lim[h, d] - TILE, logits, 0.0)
            probs = jnp.exp2(logits).astype(BF16)
            both = jnp.dot(
                probs, jnp.concatenate([earlier[:TILE, HW:], ones], axis=1),
                preferred_element_type=F32,
            )
            tot = lax.dot_general(ones8, probs, contract_last, preferred_element_type=F32)
            high = tot.astype(BF16).astype(F32)
            extra = jnp.where(row8 == 0, high, jnp.where(row8 == 1, tot - high, 0.0))
            store[h][d, :TILE] = (both[:, :HW] / both[:, HW:]).astype(BF16)
            store[h][d, TILE:] = extra.astype(BF16)

        if h == 0:
            one(0, back)

        group = 5 if h == 0 else 4

        def loop(g, carry):
            for i in range(group):
                one(1 - h + g * group + i, ret)
            for i in range(group):
                r_copy(h, 1 - h + g * group + i).start()
            return carry

        lax.fori_loop(0, (NCHIP - 1 + h) // group, loop, 0)

    def centroids(h):
        rows8 = lax.broadcasted_iota(jnp.int32, (8, HW), 0)

        def one(d, carry):
            sums, counts = carry
            cl = (t_lab[h, d] + 2) // 2 - 1
            hit = rows8 == cl
            tot = jnp.sum(recv[h][d, TILE:, :HW].astype(F32), axis=0, keepdims=True)
            sums = sums + jnp.where(hit, jnp.broadcast_to(tot, (8, HW)), 0.0)
            counts = counts + jnp.where(hit, float(TILE), 0.0)
            return sums, counts

        zero = jnp.zeros((8, HW), F32)
        sums, counts = lax.fori_loop(0, NCHIP, one, (zero, zero))
        cent = cent_ref[h]
        means = sums / jnp.maximum(counts, 1.0)
        newc_ref[h] = cent + 0.25 * jnp.where(counts > 0, means - cent, 0.0)

    def come_home(h):
        def one(d, carry):
            r_copy(h, d).wait_recv()
            return carry

        lax.fori_loop(1 - h, NCHIP, one, 0)
        for t in range(TILES):
            far = back[h][t_dst[h, t]]
            is_late = jnp.broadcast_to(late[h * TILES + t:h * TILES + t + 1, :], (TILE, HW)) > 0
            weight = lax.dot_general(
                far[TILE:], jnp.ones((8, HW), BF16), (((0,), (0,)), ((), ())),
                preferred_element_type=F32,
            )
            top = own[h][t, :, :HW] + jnp.where(is_late, weight * far[:TILE].astype(F32), 0.0)
            low = own[h][t, :, HW:] + jnp.where(is_late, weight, 0.0)
            gbuf[h, z, pl.ds(t * TILE, TILE)] = (top / low).astype(BF16)
            if t % 4 == 3:
                for way in range(2):
                    z_copy(h, way, 1, t // 4).start()

    half = TILES * TILE // 2

    def z_copy(h, way, k, j, recv_side=False):
        sign = 1 if way == 0 else -1
        at = z - sign * (k - 1)
        if recv_side:
            at = at - sign
        ref = gbuf.at[h, (at + 2 * NZ) % NZ, pl.ds(j * half, half)]
        idx = way * 8 + (k - 1) * 2 + j
        return pltpu.make_async_remote_copy(
            src_ref=ref, dst_ref=ref, send_sem=z_send.at[h, idx], recv_sem=z_recv.at[h, idx],
            device_id=((z + sign + NZ) % NZ, s), device_id_type=MESH,
        )

    def z_parts(k):
        if k < 4:
            return [(way, j) for j in range(2) for way in range(2)]
        return [(0, 0), (1, 1)]

    def z_step(h, k):
        nxt = z_parts(k + 1) if k < 4 else []
        for way, j in z_parts(k):
            z_copy(h, way, k, j, True).wait_recv()
            if (way, j) in nxt:
                z_copy(h, way, k + 1, j).start()

    def z_drain(h):
        for k in range(1, 5):
            for way, j in z_parts(k):
                z_copy(h, way, k, j).wait_send()

    def multiply(h, ga, gb, mode):
        ga = (z + ga) % NZ
        gb = (z + gb) % NZ

        rhs = jnp.concatenate([gbuf[h, ga], gbuf[h, gb]], axis=1)
        for m in range(2):
            part = slice(m * 256, (m + 1) * 256)
            lhs = jnp.concatenate([owt[h, ga, part], owt[h, gb, part]], axis=1)
            val = lax.dot_general(lhs, rhs, (((1,), (1,)), ((), ())), preferred_element_type=F32)
            if mode != "first":
                val = val + acc[m]
            if mode == "last":
                out_ref[part, :] = val.astype(BF16)
            else:
                acc[m] = val

    rest = w_steps[1][12 - lag:]
    for m in range(4):
        project(0, m)
        if m < 3 and rest:
            rest.pop(0)()
    stage_tiles(0)
    send_tiles(0)
    lateness(1)
    for f in rest:
        f()
    for m in range(4):
        project(1, m)
    send_table(1)
    stage_tiles(1)
    attend_own(0)
    tables(0)
    attend_own(1)
    tables(1)
    for j in range(4):
        not_self = (zg != z) | (s % 4 != j)

        @pl.when(not_self)
        def _(j=j):
            scattered(j).wait_recv()

    arrivals(0)
    attend(0)
    send_tiles(1)
    come_home(0)
    o_steps[0]()
    z_step(0, 1)
    o_steps[1]()
    o_steps[2]()
    z_step(0, 2)
    o_steps[3]()
    o_steps[4]()
    arrivals(1)
    attend(1)
    z_step(0, 3)
    o_steps[5]()
    o_steps[6]()
    o_steps[7]()
    come_home(1)
    for f in o_steps[8:]:
        f()
    centroids(0)
    centroids(1)
    for g in range(NZ):
        for h in range(2):
            at = (g * 2 + h) * HW
            owt[h, g] = obuf[at:at + HW, :].astype(F32).T.astype(BF16)
    z_step(0, 4)
    multiply(0, 0, 1, "first")
    z_step(1, 1)
    multiply(0, 7, 2, "mid")
    multiply(0, 6, 3, "mid")
    multiply(0, 5, 4, "mid")
    multiply(1, 1, 7, "mid")
    z_step(1, 2)
    multiply(1, 2, 6, "mid")
    z_step(1, 3)
    multiply(1, 3, 5, "mid")
    z_step(1, 4)
    multiply(1, 0, 4, "last")

    gather_w[0].drain()
    gather_w[1].drain()
    gather_o.drain()

    def codes_sent(i, carry):
        code_copy(i).wait_send()
        return carry

    lax.fori_loop(1, NSEQ, codes_sent, 0)
    for i in range(4):
        @pl.when((zg != z) | (s % 4 != i))
        def _(i=i):
            scatter(i).wait_send()

    for h in range(2):
        def sent(d, carry, h=h):
            a_copy(h, d).wait_send()
            r_copy(h, d).wait_send()
            return carry

        lax.fori_loop(1 - h, NCHIP, sent, 0)
        z_drain(h)


def on_device(tokens, qkv_weight, out_weight, centroids, clusters, slots):
    vmem = pl.BlockSpec(memory_space=pltpu.VMEM)
    dma = pltpu.SemaphoreType.DMA
    return pl.pallas_call(
        kernel,
        out_shape=(
            jax.ShapeDtypeStruct((OCOLS, TILES * TILE), BF16),
            jax.ShapeDtypeStruct(centroids.shape, F32),
        ),
        in_specs=[
            vmem, vmem,
            pl.BlockSpec(memory_space=pl.ANY),
            vmem, vmem, vmem,
        ],
        out_specs=(vmem, vmem),
        scratch_shapes=[
            pltpu.VMEM(tokens.shape, BF16),
            pltpu.VMEM((NSEQ * WROWS, 2 * QKV), BF16),
            pltpu.VMEM((NSEQ * OROWS, OCOLS), BF16),
            pltpu.VMEM((2, NZ, OCOLS, HW), BF16),
            pltpu.VMEM((TILES * TILE, 128), F32),
        ]
        + [pltpu.VMEM((TILES, TILE, QKV), BF16)] * 2
        + [pltpu.VMEM((NCHIP, MROWS, 2 * HW), BF16)] * 4
        + [pltpu.VMEM((NCHIP, MROWS, HW), BF16)] * 4
        + [
            pltpu.VMEM((2, NZ, TILES * TILE, HW), BF16),
            pltpu.VMEM((2, 256, TILES * TILE), F32),
        ]
        + [pltpu.VMEM((TILES, MROWS, 2 * HW), BF16)] * 2
        + [pltpu.VMEM((TILES, TILE, 2 * HW), F32)] * 2
        + [pltpu.VMEM((2 * TILES, 128), jnp.int32)]
        + [pltpu.SMEM((NSEQ, 2, 128), jnp.int32), pltpu.VMEM((NSEQ, 2, 128), jnp.int32)]
        + [pltpu.SMEM((2, NCHIP), jnp.int32)] * 5
        + [pltpu.SMEM((2, TILES), jnp.int32)]
        + [
            dma((TILES,)), dma((2, 36)), dma((2, 36)), dma((36,)), dma((36,)),
            dma((4,)), dma((4,)), dma,
            dma((2, NCHIP)), dma((2, NCHIP)), dma((2, NCHIP)), dma((2, NCHIP)),
            dma((2, 16)), dma((2, 16)), dma((NSEQ,)), dma((NSEQ,)),
        ],
        compiler_params=pltpu.CompilerParams(
            collective_id=0, has_side_effects=True, vmem_limit_bytes=60 * 1024 * 1024
        ),
    )(clusters, slots, tokens, qkv_weight, out_weight, centroids)


def solution(mesh):
    return jax.shard_map(
        on_device,
        mesh=mesh,
        in_specs=(
            P("seq", None),
            P("seq", "head"),
            P("head", "seq"),
            P("head", "seq", None),
            P("head", "seq"),
            P("head", "seq"),
        ),
        out_specs=(P("head", "seq"), P("head", "seq", None)),
        check_vma=False,
    )
```
